512 devices in a mesh: xy: 64 (over x, y, core), gz: 8 (over z).
Axes of the slice: x: 4, y: 8, z: 8, core: 2. Of those that a mesh axis runs over, the one named last changes fastest.
Arguments:
- potential_temp: float32 [16, 256, 512], P('gz', 'xy'), may hold values from -6 to 6
- wind_field: float32 [3, 16, 256, 512], P(None, 'gz', 'xy'), may hold values from -0.25 to 0.25
- eddy_diff: float32 [16, 256, 512], P('gz', 'xy'), may hold values from 0.005 to 0.04
- facade_cell: int32 [8, 8192, 128], P('gz', 'xy'), may hold values from 0 to 4095
- tile_send: int32 [8, 8192], P('gz', 'xy'), may hold values from -1 to 127, as said below
- tile_take: int32 [8, 4096], P('gz', 'xy'), may hold values from 0 to 127, as said below
- wall_temp: float32 [8, 4096, 32, 128], P('gz', 'xy'), may hold values from -6 to 6
- wall_class: int32 [8, 4096], P('gz', 'xy'), may hold values from 0 to 3
- wall_inverse: float32 [4, 32, 32], replicated, as said below
- refl_block: bfloat16 [64, 128, 128, 128], P('xy', 'gz'), may hold values from -0.5 to 0.5
- refl_pair: int32 [64, 2, 128], P('xy', None, 'gz'), may hold values from 0 to 511
Outputs:
- temp_next: float32 [16, 256, 512], P('gz', 'xy')
- wall_next: float32 [8, 4096, 32, 128], P('gz', 'xy')
The draws below stay inside these ranges and needn't reach their ends.
Inputs may be any that keep to these rules, and one draw needn't show every extreme that they name: `tile_send`: in each vertical index, each LES device's live slots carry distinct values dest * 2 + c with c below the number of tiles that it sends to owner dest, and at most 2 tiles go from one LES device to one owner; some LES device has all 128 slots live, with 2 tiles to every owner, and empty slots hold -1. `tile_take`: for owner j at vertical index k, the 64 values are exactly the rows src * 2 + c for which LES device src sends a tile with value j * 2 + c, each once; every owner receives exactly 64 tiles. `wall_inverse`: nonnegative entries, diagonally dominant by rows.
All inputs are finite; a program needn't handle non-finite values.
Results may differ from the reference program's by a relative error of at most 0.0014.
Values may be sent and summed in bfloat16 or wider, within the bound.
No kernel may reach another device: no remote copies, remote signals or barrier semaphores. Data moves between devices by JAX's collectives and lax.ppermute only.
A program may use at most 64 MiB of HBM per device.

```python
import math
import jax
import jax.numpy as jnp
from jax import lax

CZ = 2
CX = 4
NY = 512
TILE = 128
NODES = 32
NMAT = 4
SUB = 4
OWN = 64
NB = 16
TMAX = 128
CAP = 2
NZ = 16
NX = 256
N_XY = 64
N_GZ = 8


def routing_level(level_key):
    pair_count = N_XY // 2
    order = jax.random.permutation(jax.random.fold_in(level_key, 1), N_XY).astype(jnp.int32)
    at_end = ((order == 0) | (order == N_XY - 1)).astype(jnp.int32)
    order = order[jnp.argsort(at_end * N_XY + jnp.arange(N_XY, dtype=jnp.int32))]
    first_rows = order[0::2]
    second_rows = order[1::2]
    bias = jax.random.randint(jax.random.fold_in(level_key, 2), (pair_count, 1, 1), 250, 751)
    coin = jax.random.randint(jax.random.fold_in(level_key, 3), (pair_count, N_XY, CAP), 0, 1000)
    counts_first = jnp.sum((coin < bias).astype(jnp.int32), axis=2)
    high_col = jax.random.randint(jax.random.fold_in(level_key, 4), (pair_count,), 0, N_XY)
    low_col = (high_col + 1 + jax.random.randint(jax.random.fold_in(level_key, 5), (pair_count,), 0, N_XY - 1)) % N_XY
    columns = jnp.arange(N_XY, dtype=jnp.int32)[None, :]
    counts_first = jnp.where(columns == high_col[:, None], CAP, counts_first)
    counts_first = jnp.where(columns == low_col[:, None], 0, counts_first)
    full_pair = (jnp.arange(pair_count) == 0)[:, None]
    counts_first = jnp.where(full_pair, CAP, counts_first).astype(jnp.int32)
    counts_second = (CAP - counts_first).astype(jnp.int32)
    matrix = jnp.zeros((N_XY, N_XY), jnp.int32).at[first_rows].set(counts_first).at[second_rows].set(counts_second)
    return matrix


def send_level(level_key, matrix):
    cumulative = jnp.cumsum(matrix, axis=1)
    live_count = cumulative[:, -1]
    ranks = jnp.arange(TMAX, dtype=jnp.int32)
    destination = jnp.sum((cumulative[:, None, :] <= ranks[None, :, None]).astype(jnp.int32), axis=2)
    destination = jnp.minimum(destination, N_XY - 1)
    before = jnp.take_along_axis(cumulative - matrix, destination, axis=1)
    place = ranks[None, :] - before
    values = jnp.where(ranks[None, :] < live_count[:, None], destination * CAP + place, -1).astype(jnp.int32)
    slot_keys = jax.random.split(jax.random.fold_in(level_key, 6), N_XY)
    slot_order = jax.vmap(lambda one_key: jax.random.permutation(one_key, TMAX))(slot_keys).astype(jnp.int32)
    device_ids = jnp.arange(N_XY, dtype=jnp.int32)[:, None]
    rows = jnp.zeros((N_XY, TMAX), jnp.int32).at[device_ids, slot_order].set(values)
    return rows.reshape(N_XY * TMAX)


def take_level(level_key, matrix):
    index = jnp.arange(N_XY * CAP, dtype=jnp.int32)
    source = index // CAP
    place = index % CAP
    valid = (place[None, :] < jnp.transpose(matrix)[:, source]).astype(jnp.int32)
    score = (1 - valid) * (N_XY * CAP) + index[None, :]
    chosen = jnp.argsort(score, axis=1)[:, :OWN].astype(jnp.int32)
    home_keys = jax.random.split(jax.random.fold_in(level_key, 7), N_XY)
    home_order = jax.vmap(lambda one_key: jax.random.permutation(one_key, OWN))(home_keys).astype(jnp.int32)
    result = jnp.take_along_axis(chosen, home_order, axis=1)
    return result.reshape(N_XY * OWN).astype(jnp.int32)


def level_lists(key):

    def one_level(level):
        level_key = jax.random.fold_in(key, 1000 + level)
        matrix = routing_level(level_key)
        return (send_level(level_key, matrix), take_level(level_key, matrix))
    return jax.vmap(one_level)(jnp.arange(N_GZ, dtype=jnp.int32))


def draw_tile_send(key, part):
    return level_lists(key)[0]


def draw_tile_take(key, part):
    return level_lists(key)[1]


def draw_wall_inverse(key, part):
    main_part = jax.random.uniform(jax.random.fold_in(key, 11), (NMAT, NODES, NODES), jnp.float32, 0.4, 0.8)
    side_part = jax.random.uniform(jax.random.fold_in(key, 12), (NMAT, NODES, NODES), jnp.float32, 0.0, 0.5 / NODES)
    row_ids = lax.broadcasted_iota(jnp.int32, (NMAT, NODES, NODES), 1)
    col_ids = lax.broadcasted_iota(jnp.int32, (NMAT, NODES, NODES), 2)
    return jnp.where(row_ids == col_ids, main_part, side_part)


def plant(drawn, stream_key, least, top_value):
    extent = drawn.shape
    index_at = [jax.random.randint(jax.random.fold_in(stream_key, axis), (), 0, extent[axis]) for axis in range(len(extent))]
    drawn = drawn.at[tuple(index_at)].set(least)
    longest = extent.index(max(extent))
    index_at[longest] = (index_at[longest] + 1) % extent[longest]
    return drawn.at[tuple(index_at)].set(top_value)


def level_of(key, shape, shards, least, high):
    level, own = 1.0, jax.random.fold_in(key, 6)
    for axis_at, parts in shards:
        draws = jnp.exp(jax.random.uniform(jax.random.fold_in(own, axis_at), (parts,), jnp.float32, least / len(shards), high / len(shards)))
        level = level * jnp.repeat(draws, shape[axis_at] // parts).reshape([-1 if axis == axis_at else 1 for axis in range(len(shape))])
    return level


def gaussian(rng, extent, deviation, reach, pieces=(), kind=jnp.bfloat16):
    array = deviation * jax.random.normal(rng, extent, jnp.float32)
    if pieces:
        array = array * level_of(rng, extent, pieces, -0.22, 0.18)
    return jnp.clip(array, -reach, reach).astype(kind)


def setup_inputs(seed: int = 0) -> dict:
    keys = jax.random.split(jax.random.key(seed), 12)
    potential_temp = gaussian(keys[0], (NZ, NX, NY), 1.0, 6.0, ((0, 8), (1, 64)), jnp.float32)
    wind_field = jnp.clip(jax.random.uniform(keys[1], (3, NZ, NX, NY), jnp.float32, -0.25, 0.25) * level_of(keys[1], (3, NZ, NX, NY), ((1, 8), (2, 64)), -0.4, 0.0), -0.25, 0.25)
    eddy_diff = jnp.clip(jnp.exp(math.log(0.04) - 2.0794415 * jax.random.uniform(keys[2], (NZ, NX, NY), jnp.float32) ** level_of(keys[2], (NZ, NX, NY), ((0, 8), (1, 64)), -0.2, 0.2)), 0.005, 0.04)
    facade_cell = plant(jax.random.randint(keys[3], (N_GZ, N_XY * TMAX, TILE), 0, CZ * CX * NY), jax.random.fold_in(keys[3], 1), 0, (CZ * CX * NY) - 1).astype(jnp.int32)
    tile_send = draw_tile_send(jax.random.fold_in(keys[11], 71), 0)
    tile_take = draw_tile_take(jax.random.fold_in(keys[11], 71), 0)
    wall_temp = gaussian(keys[6], (N_GZ, N_XY * OWN, NODES, TILE), 1.0, 6.0, ((0, 8), (1, 64)), jnp.float32)
    wall_class = plant(jax.random.randint(keys[7], (N_GZ, N_XY * OWN), 0, NMAT), jax.random.fold_in(keys[7], 1), 0, NMAT - 1).astype(jnp.int32)
    wall_inverse = draw_wall_inverse(jax.random.fold_in(keys[11], 71), 0)
    refl_block = gaussian(keys[9], (N_XY, N_GZ * NB, TILE, TILE), TILE ** -0.5, 0.5, ((0, 64), (1, 8)))
    refl_pair = plant(jax.random.randint(keys[10], (N_XY, 2, N_GZ * NB), 0, N_GZ * OWN), jax.random.fold_in(keys[10], 1), 0, (N_GZ * OWN) - 1).astype(jnp.int32)
    return {"potential_temp": potential_temp, "wind_field": wind_field, "eddy_diff": eddy_diff, "facade_cell": facade_cell, "tile_send": tile_send, "tile_take": tile_take, "wall_temp": wall_temp, "wall_class": wall_class, "wall_inverse": wall_inverse, "refl_block": refl_block, "refl_pair": refl_pair}


wall_gain = 0.25
flux_gain = 0.5


def upwind(speed, centre, lower, upper):
    return jnp.maximum(speed, 0.0) * (centre - lower) + jnp.minimum(speed, 0.0) * (upper - centre)


def to_devices(field):
    cell_count = CZ * CX * NY
    return field.reshape(N_GZ, CZ, N_XY, CX, NY).transpose(0, 2, 1, 3, 4).reshape(N_GZ, N_XY, cell_count)


def from_devices(field):
    return field.reshape(N_GZ, N_XY, CZ, CX, NY).transpose(0, 2, 1, 3, 4).reshape(NZ, NX, NY)


def district_sum(inputs):
    blocks, pair_rows, emitted = inputs
    source_emit = emitted[pair_rows[1]].astype(jnp.float32)
    contrib = jnp.einsum("bij,bj->bi", blocks.astype(jnp.float32), source_emit)
    return jnp.zeros((N_GZ * OWN, TILE), jnp.float32).at[pair_rows[0]].add(contrib)


def reference(potential_temp, wind_field, eddy_diff, facade_cell, tile_send, tile_take, wall_temp, wall_class, wall_inverse, refl_block, refl_pair):
    slot_total = N_XY * CAP
    speed_sq = wind_field[0] * wind_field[0] + wind_field[1] * wind_field[1] + wind_field[2] * wind_field[2]
    theta_dev = to_devices(potential_temp)
    speed_dev = to_devices(speed_sq)
    cell_index = facade_cell.reshape(N_GZ, N_XY, TMAX * TILE)
    air_slots = jnp.take_along_axis(theta_dev, cell_index, axis=2).reshape(N_GZ, N_XY, TMAX, TILE)
    coef_slots = 0.5 + 4.0 * jnp.take_along_axis(speed_dev, cell_index, axis=2).reshape(N_GZ, N_XY, TMAX, TILE)
    send_rows = tile_send.reshape(N_GZ, N_XY, TMAX)
    level_ids = jnp.arange(N_GZ, dtype=jnp.int32)[:, None, None]
    device_ids = jnp.arange(N_XY, dtype=jnp.int32)[None, :, None]
    target_rows = jnp.where(send_rows >= 0, send_rows, slot_total)
    empty_box = jnp.zeros((N_GZ, N_XY, slot_total + 1, TILE), potential_temp.dtype)
    air_out = empty_box.at[level_ids, device_ids, target_rows].set(air_slots)[:, :, :slot_total]
    coef_out = empty_box.at[level_ids, device_ids, target_rows].set(coef_slots)[:, :, :slot_total]
    take_rows = tile_take.reshape(N_GZ, N_XY, OWN)
    source_dev = take_rows // CAP
    source_col = take_rows % CAP
    own_air = air_out[level_ids, source_dev, device_ids * CAP + source_col]
    own_coef = coef_out[level_ids, source_dev, device_ids * CAP + source_col]
    wall_state = wall_temp.reshape(N_GZ, N_XY, OWN, NODES, TILE)
    emitted = wall_state[:, :, :, 0, :].astype(jnp.bfloat16)
    district_emit = emitted.transpose(1, 0, 2, 3).reshape(N_XY, N_GZ * OWN, TILE)
    reflected = lax.map(district_sum, (refl_block, refl_pair, district_emit))
    own_rad = reflected.reshape(N_XY, N_GZ, OWN, TILE).transpose(1, 0, 2, 3)
    inverse_tile = wall_inverse[wall_class.reshape(N_GZ, N_XY, OWN)]
    temps = wall_state
    for substep in range(SUB):
        forcing = own_coef * (own_air - temps[:, :, :, 0, :]) + own_rad
        temps = temps.at[:, :, :, 0, :].add(wall_gain * forcing)
        temps = jnp.einsum("kjhab,kjhbf->kjhaf", inverse_tile, temps, precision=lax.Precision.HIGHEST)
    flux_out = own_coef * (temps[:, :, :, 0, :] - own_air)
    back_rows = jnp.zeros((N_GZ, N_XY, slot_total, TILE), potential_temp.dtype)
    back_rows = back_rows.at[level_ids, source_dev, device_ids * CAP + source_col].set(flux_out)
    slot_flux = back_rows[level_ids, device_ids, jnp.maximum(send_rows, 0)]
    slot_flux = jnp.where((send_rows >= 0)[:, :, :, None], slot_flux, 0.0)
    heat_dev = jnp.zeros((N_GZ, N_XY, CZ * CX * NY), potential_temp.dtype)
    heat_dev = heat_dev.at[level_ids, device_ids, cell_index].add(slot_flux.reshape(N_GZ, N_XY, TMAX * TILE))
    heat_cells = from_devices(heat_dev)
    centre = potential_temp
    padded = jnp.pad(centre, ((1, 1), (1, 1), (0, 0)))
    lower_z = padded[:-2, 1:-1]
    upper_z = padded[2:, 1:-1]
    lower_x = padded[1:-1, :-2]
    upper_x = padded[1:-1, 2:]
    lower_y = jnp.roll(centre, 1, axis=2)
    upper_y = jnp.roll(centre, -1, axis=2)
    advect = upwind(wind_field[0], centre, lower_z, upper_z) + upwind(wind_field[1], centre, lower_x, upper_x) + upwind(wind_field[2], centre, lower_y, upper_y)
    laplace = (lower_z + upper_z + lower_x + upper_x + lower_y + upper_y) - 6.0 * centre
    temp_next = centre - advect + eddy_diff * laplace + flux_gain * heat_cells
    return temp_next, temps.reshape(N_GZ, N_XY * OWN, NODES, TILE)
```

```python
import functools

import jax
import jax.numpy as jnp
from jax import lax
from jax.experimental import pallas as pl
from jax.experimental.pallas import tpu as pltpu
from jax.sharding import PartitionSpec as P


wall_gain = 0.25
flux_gain = 0.5
FULL = 60 << 20
air_step = 6.0 / 32640.0
coef_step = 0.75 / 32640.0

F32 = jnp.float32
BF16 = jnp.bfloat16
VMEM = pl.BlockSpec(memory_space=pltpu.VMEM)
HBM = pl.BlockSpec(memory_space=pltpu.HBM)
SMEM = pl.BlockSpec(memory_space=pltpu.SMEM)


def sds(shape, dtype):
    return jax.ShapeDtypeStruct(shape, dtype)


def call(body, in_specs, outs, args, scratch=(), flops=0, nbytes=1 << 20, limit=12 << 20):
    return pl.pallas_call(
        body,
        in_specs=in_specs,
        out_specs=tuple(VMEM for _ in outs),
        out_shape=tuple(outs),
        scratch_shapes=list(scratch),
        compiler_params=pltpu.CompilerParams(vmem_limit_bytes=limit),
        cost_estimate=pl.CostEstimate(flops=flops, bytes_accessed=nbytes, transcendentals=0),
    )(*args)


def iota(shape, dim):
    return lax.broadcasted_iota(jnp.int32, shape, dim)


def dot(lhs, rhs, dims=((1,), (0,))):
    return lax.dot_general(lhs, rhs, (dims, ((), ())), preferred_element_type=F32)


def column(row, size):
    picked = jnp.where(iota((size, size), 0) == iota((size, size), 1), row, 0.0)
    return jnp.sum(picked, axis=1, keepdims=True)


def split(value):
    high = value.astype(BF16)
    return high, (value - high.astype(F32)).astype(BF16)


def code(value):
    whole = jnp.round(value)
    high = jnp.floor(whole * (1.0 / 256.0))
    return high.astype(BF16), (whole - 256.0 * high).astype(BF16)


def pack_body(wall_ref, pair_ref, theta_ref, out_ref, node_ref, near_ref, level_ref, ids_ref, plane_ref, sems):
    copies = [
        pltpu.make_async_copy(wall_ref.at[0, :, 0, :], node_ref, sems.at[0]),
        pltpu.make_async_copy(pair_ref, near_ref, sems.at[1]),
        pltpu.make_async_copy(theta_ref, level_ref, sems.at[2]),
    ]
    for copy in copies:
        copy.start()
    level = lax.axis_index("gz")
    parts = out_ref.shape[0]
    owned = node_ref.shape[0]
    ids_ref[...] = jnp.full(ids_ref.shape, -1.0, F32)
    for copy in copies:
        copy.wait()
    target = near_ref[0, 0:1, :]
    blocks = target.shape[1]
    for side in range(2):
        for q in range(4):
            plane_ref[side, 4 * q : 4 * q + 4, :] = level_ref[side, :, 128 * q : 128 * q + 128]
    emitted = node_ref[...].astype(BF16)
    for dest in range(parts):
        near = target - dest * owned
        inside = (near >= 0) & (near < owned)
        ids_ref[0:1, 0:blocks] = jnp.where(inside, near, -1).astype(F32)
        up = jnp.where(level + 1 == dest, plane_ref[1], 0.0)
        down = jnp.where(level - 1 == dest, plane_ref[0], 0.0)
        out_ref[dest, 0:owned, :] = emitted
        out_ref[dest, owned : owned + 16, :] = ids_ref[...].astype(BF16)
        out_ref[dest, owned + 16 : owned + 32, :] = (up + down).astype(BF16)


def lookup_body(theta_ref, wind_ref, cell_ref, send_ref, air_ref, speed_ref, out_ref, theta_tab, speed_tab):
    theta = jnp.concatenate([theta_ref[0], theta_ref[1]], axis=0)
    speed = jnp.zeros_like(theta)
    for d in range(3):
        w = jnp.concatenate([wind_ref[d, 0], wind_ref[d, 1]], axis=0)
        speed = speed + w * w
    for q in range(4):
        theta_tab[8 * q : 8 * q + 8, :] = theta[:, 128 * q : 128 * q + 128]
        speed_tab[8 * q : 8 * q + 8, :] = 4.0 * speed[:, 128 * q : 128 * q + 128]
    slots = cell_ref.shape[0]

    def group(p, carry):
        base = pl.multiple_of(p * 8, 8)
        cells = cell_ref[pl.ds(base, 8), :]
        lane = cells & 127
        line = ((cells >> 7) & 3) * 8 + (cells >> 9)
        air = jnp.zeros((8, 128), F32)
        spd = jnp.zeros((8, 128), F32)
        for r in range(32):
            here = line == r
            for_air = jnp.broadcast_to(theta_tab[r : r + 1, :], (8, 128))
            for_spd = jnp.broadcast_to(speed_tab[r : r + 1, :], (8, 128))
            for_air = jnp.take_along_axis(for_air, lane, axis=1, mode="promise_in_bounds")
            for_spd = jnp.take_along_axis(for_spd, lane, axis=1, mode="promise_in_bounds")
            air = jnp.where(here, for_air, air)
            spd = jnp.where(here, for_spd, spd)
        air_ref[pl.ds(base, 8), :] = air
        speed_ref[pl.ds(base, 8), :] = spd
        return carry

    lax.fori_loop(0, slots // 8, group, 0, unroll=8)
    rows = iota((2 * slots, slots), 0)
    wanted = (rows >> 2) * 2 + (rows & 1)
    is_speed = ((rows >> 1) & 1) == 1
    hit = send_ref[...] == wanted
    pick_air = jnp.where(hit & jnp.logical_not(is_speed), 1.0, 0.0).astype(BF16)
    pick_speed = jnp.where(hit & is_speed, 1.0, 0.0).astype(BF16)
    air_high, air_low = code(air_ref[...] * (1.0 / air_step))
    speed_high, speed_low = code(speed_ref[...] * (1.0 / coef_step))
    out = 256.0 * (dot(pick_air, air_high) + dot(pick_speed, speed_high))
    out = out + (dot(pick_air, air_low) + dot(pick_speed, speed_low))
    out_ref[...] = out.astype(jnp.int32).astype(jnp.int16)


def reflect_body(pair_ref, recv_ref, block_ref, out_ref, add_ref, all_ref, src_ref):
    parts, owned, blocks = recv_ref.shape[0], add_ref.shape[0], block_ref.shape[1]
    lane = iota((1, 128), 1)
    ids = jnp.zeros((1, 128), F32)
    for part in range(parts):
        all_ref[part * owned : (part + 1) * owned, :] = recv_ref[part, 0:owned, :].astype(F32)
        row = recv_ref[part, owned : owned + 16, :].astype(F32)[0:1, :]
        row = jnp.where(lane < blocks, row, 0.0)
        ids = ids + (pltpu.roll(row, part * blocks, 1) if part else row)
    for b in range(blocks):
        src_ref[b : b + 1, :] = all_ref[pl.ds(pair_ref[0, 1, b], 1), :]
    source = src_ref[...].astype(BF16)
    which = iota((blocks, 128), 0)
    total = jnp.zeros((blocks, 128), F32)
    for b in range(blocks):
        one = dot(source, block_ref[0, b], ((1,), (1,)))
        total = jnp.where(which == b, one, total)
    for part in range(parts):
        out_ref[part] = total.astype(BF16)
    hot = iota(add_ref.shape, 0).astype(F32) == ids
    add_ref[...] = jnp.where(hot, 1.0, 0.0).astype(BF16)


def wall_body(
    class_ref, inverse_ref, wall_ref, take_ref, free_ref, rows_ref, gain_ref, resp_ref, take_out, back_out, lhs_ref,
):
    nodes = inverse_ref.shape[1]
    full = functools.partial(
        lax.dot_general,
        dimension_numbers=(((1,), (0,)), ((), ())),
        precision=lax.Precision.HIGHEST,
        preferred_element_type=F32,
    )
    for c in range(inverse_ref.shape[0]):
        one = inverse_ref[c]
        two = full(one, one)
        three = full(two, one)
        four = full(two, two)
        stack = jnp.concatenate(
            [four, one[0:1], two[0:1], three[0:1], jnp.zeros((13, nodes), F32)], axis=0
        )
        high, low = split(stack)
        lhs_ref[c] = jnp.concatenate([high, high, low], axis=1)
        for k, power in enumerate((one, two, three, four)):
            resp_ref[c, k] = jnp.broadcast_to(power[:, 0:1], (nodes, 128))

    owned = wall_ref.shape[1]

    def tiles(g, carry):
        base = pl.multiple_of(g * 8, 8)
        firsts = [[], [], [], [], []]
        gains = [[], [], [], []]
        for q in range(8):
            t = base + q
            kind = class_ref[0, t]
            state = wall_ref[0, t]
            high, low = split(state)
            result = dot(lhs_ref[kind], jnp.concatenate([high, low, high], axis=0))
            free_ref[t] = result[0:nodes]
            for k in range(3):
                firsts[k].append(result[nodes + k : nodes + k + 1])
            firsts[3].append(state[0:1])
            firsts[4].append(result[0:1])
            for k in range(4):
                gains[k].append(resp_ref[kind, k, 0:1, :])
        for k in range(5):
            rows_ref[k, pl.ds(base, 8), :] = jnp.concatenate(firsts[k], axis=0)
        for k in range(4):
            gain_ref[k, pl.ds(base, 8), :] = jnp.concatenate(gains[k], axis=0)
        return carry

    lax.fori_loop(0, owned // 8, tiles, 0, unroll=2)
    take = take_ref[...]
    col = column(take.astype(F32), owned).astype(jnp.int32)
    place = (col >> 1) * 4 + (col & 1)
    lanes = iota((owned, take_out.shape[1]), 1)
    take_out[0:owned, :] = jnp.where(lanes == place, 1.0, 0.0).astype(BF16)
    take_out[owned : 2 * owned, :] = jnp.where(lanes == place + 2, 1.0, 0.0).astype(BF16)
    back_out[...] = jnp.where(iota((2 * owned, owned), 0) == take, 1.0, 0.0).astype(BF16)


def force_body(recv_ref, take_ref, back_ref, refl_ref, add_ref, rows_ref, gain_ref, force_ref, out_ref):
    owned = add_ref.shape[0]
    high, low = code(recv_ref[...].astype(jnp.int32).astype(F32))
    both = 256.0 * dot(take_ref[...], high) + dot(take_ref[...], low)
    air = air_step * both[0:owned]
    coef = 0.5 + coef_step * both[owned : 2 * owned]
    parts, blocks = refl_ref.shape[0], refl_ref.shape[1]
    rad = dot(add_ref[...], refl_ref[...].reshape(parts * blocks, 128))
    g1, g2, g3, g4 = gain_ref[0], gain_ref[1], gain_ref[2], gain_ref[3]
    f0 = wall_gain * (coef * (air - rows_ref[3]) + rad)
    f1 = wall_gain * (coef * (air - (rows_ref[0] + g1 * f0)) + rad)
    f2 = wall_gain * (coef * (air - (rows_ref[1] + (g2 * f0 + g1 * f1))) + rad)
    f3 = wall_gain * (coef * (air - (rows_ref[2] + (g3 * f0 + g2 * f1 + g1 * f2))) + rad)
    force_ref[0] = f0
    force_ref[1] = f1
    force_ref[2] = f2
    force_ref[3] = f3
    surface = rows_ref[4] + (g4 * f0 + g3 * f1 + g2 * f2 + g1 * f3)
    high, low = split(surface)
    out_ref[...] = dot(back_ref[...], high) + dot(back_ref[...], low)


def upwind(speed, centre, lower, upper):
    return jnp.maximum(speed, 0.0) * (centre - lower) + jnp.minimum(speed, 0.0) * (upper - centre)


def finish_body(
    class_ref, free_ref, force_ref, resp_ref, send_ref, speed_ref, theta_ref, wind_ref, eddy_ref, zhalo_ref,
    before_ref, after_ref, out_ref, pick_ref, coef_ref, base_ref,
):
    def tile(t, carry):
        kind = class_ref[0, t]
        value = free_ref[t]
        for k in range(4):
            value = value + resp_ref[kind, 3 - k] * force_ref[k, pl.ds(t, 1), :]
        out_ref[0, t] = value
        return carry

    lax.fori_loop(0, free_ref.shape[0], tile, 0, unroll=4)
    slots = send_ref.shape[1]
    slot_col = column(send_ref[...].astype(F32), slots)
    pick_ref[...] = jnp.where(iota((slots, slots), 1).astype(F32) == slot_col, 1.0, 0.0).astype(BF16)
    coef_ref[...] = jnp.where(slot_col >= 0.0, 0.5 + speed_ref[...], 0.0)
    level = lax.axis_index("gz")
    parts = zhalo_ref.shape[0]

    def plane(from_part, valid):
        value = zhalo_ref[jnp.clip(from_part, 0, parts - 1)].astype(F32)
        value = jnp.concatenate([value[4 * q : 4 * q + 4] for q in range(4)], axis=1)
        return jnp.where(valid, value, 0.0)

    below = plane(level - 1, level > 0)
    above = plane(level + 1, level < parts - 1)
    for k in range(2):
        c = theta_ref[k]
        lower_z = theta_ref[0] if k else below
        upper_z = above if k else theta_ref[1]
        lower_x = jnp.concatenate([before_ref[k], c[0:3]], axis=0)
        upper_x = jnp.concatenate([c[1:4], after_ref[k]], axis=0)
        lower_y = jnp.concatenate([c[:, -1:], c[:, :-1]], axis=1)
        upper_y = jnp.concatenate([c[:, 1:], c[:, :1]], axis=1)
        advect = (
            upwind(wind_ref[0, k], c, lower_z, upper_z)
            + upwind(wind_ref[1, k], c, lower_x, upper_x)
            + upwind(wind_ref[2, k], c, lower_y, upper_y)
        )
        laplace = lower_z + upper_z + lower_x + upper_x + lower_y + upper_y - 6.0 * c
        base_ref[k] = c - advect + eddy_ref[k] * laplace


def deposit_body(recv_ref, pick_ref, air_ref, coef_ref, cell_ref, base_ref, out_ref, flux_ref, acc_ref):
    slots = cell_ref.shape[0]
    high, low = split(recv_ref[...])
    surface = dot(pick_ref[...], high) + dot(pick_ref[...], low)
    flux_ref[...] = coef_ref[...] * (surface - air_ref[...])
    count = 8
    lanes = iota((128, count * 128), 0).astype(BF16)
    lines = iota((32, count * 128), 0).astype(BF16)
    acc_ref[...] = jnp.zeros_like(acc_ref)

    def flat(rows):
        return jnp.concatenate([rows[i : i + 1] for i in range(count)], axis=1)

    def group(p, carry):
        base = pl.multiple_of(p * count, count)
        cells = cell_ref[pl.ds(base, count), :]
        lane = flat((cells & 127).astype(F32)).astype(BF16)
        line = flat((((cells >> 7) & 3) * 8 + (cells >> 9)).astype(F32)).astype(BF16)
        high, low = split(flat(flux_ref[pl.ds(base, count), :]))
        hot = jnp.where(lanes == lane, BF16(1), BF16(0))
        here = lines == line
        placed = jnp.concatenate([jnp.where(here, high, BF16(0)), jnp.where(here, low, BF16(0))], axis=0)
        acc_ref[...] += dot(hot, placed, ((1,), (1,)))
        return carry

    lax.fori_loop(0, slots // count, group, 0, unroll=8)
    heat = acc_ref[...].T
    heat = heat[0:32] + heat[32:64]
    heat = jnp.concatenate([heat[8 * q : 8 * q + 8] for q in range(4)], axis=1)
    for k in range(2):
        out_ref[k] = base_ref[k] + flux_gain * heat[4 * k : 4 * k + 4]


def on_device(
    potential_temp,
    wind_field,
    eddy_diff,
    facade_cell,
    tile_send,
    tile_take,
    wall_temp,
    wall_class,
    wall_inverse,
    refl_block,
    refl_pair,
):
    slots = facade_cell.shape[1]
    owned = tile_take.shape[1]
    nodes = wall_temp.shape[2]
    classes = wall_inverse.shape[0]
    blocks = refl_block.shape[1]
    parts = lax.axis_size("gz")
    xy_count = lax.axis_size("xy")
    cells = facade_cell.reshape(slots, 128)
    dma = pltpu.SemaphoreType.DMA

    (payload,) = call(
        pack_body,
        [HBM] * 3,
        [sds((parts, owned + 32, 128), BF16)],
        (wall_temp, refl_pair, potential_temp),
        [
            pltpu.VMEM((owned, 128), F32),
            pltpu.VMEM(refl_pair.shape, jnp.int32),
            pltpu.VMEM(potential_temp.shape, F32),
            pltpu.VMEM((16, 128), F32),
            pltpu.VMEM((2, 16, 128), F32),
            dma((3,)),
        ],
        limit=FULL,
    )
    district = lax.all_to_all(payload, "gz", split_axis=0, concat_axis=0, tiled=True)

    air, speed, send_list = call(
        lookup_body,
        [VMEM] * 4,
        [sds((slots, 128), F32), sds((slots, 128), F32), sds((2 * slots, 128), jnp.int16)],
        (potential_temp, wind_field, cells, tile_send),
        [pltpu.VMEM((32, 128), F32), pltpu.VMEM((32, 128), F32)],
        flops=2 * 48 * 256 * slots * 128,
    )
    free, rows, gain, resp, take_pick, back_pick = call(
        wall_body,
        [SMEM] + [VMEM] * 3,
        [
            sds((owned, nodes, 128), F32),
            sds((5, owned, 128), F32),
            sds((4, owned, 128), F32),
            sds((classes, 4, nodes, 128), F32),
            sds((2 * owned, 2 * slots), BF16),
            sds((2 * owned, owned), BF16),
        ],
        (wall_class, wall_inverse, wall_temp, tile_take),
        [pltpu.VMEM((classes, nodes + 16, 3 * nodes), BF16)],
        flops=2 * 48 * 96 * owned * 128,
    )
    send_list, district, rows = lax.optimization_barrier((send_list, district, rows))
    received = lax.all_to_all(send_list, "xy", split_axis=0, concat_axis=0, tiled=True)

    last = xy_count - 1
    before = lax.ppermute(potential_temp[:, 3:4, :], "xy", [(i, i + 1) for i in range(last)])
    after = lax.ppermute(potential_temp[:, 0:1, :], "xy", [(i + 1, i) for i in range(last)])

    contrib, add_matrix = call(
        reflect_body,
        [SMEM, VMEM, VMEM],
        [sds((parts, blocks, 128), BF16), sds((owned, 128), BF16)],
        (refl_pair, district, refl_block),
        [pltpu.VMEM((parts * owned, 128), F32), pltpu.VMEM((blocks, 128), F32)],
    )
    contrib, received = lax.optimization_barrier((contrib, received))
    reflected = lax.all_to_all(contrib, "gz", split_axis=0, concat_axis=0, tiled=True)

    force, back_list = call(
        force_body,
        [VMEM] * 7,
        [sds((4, owned, 128), F32), sds((2 * owned, 128), F32)],
        (received, take_pick, back_pick, reflected, add_matrix, rows, gain),
    )
    returned = lax.all_to_all(back_list, "xy", split_axis=0, concat_axis=0, tiled=True)
    wall_next, pick, coef, base = call(
        finish_body,
        [SMEM] + [VMEM] * 11,
        [
            sds((1, owned, nodes, 128), F32),
            sds((slots, slots), BF16),
            sds((slots, 128), F32),
            sds(potential_temp.shape, F32),
        ],
        (
            wall_class, free, force, resp, tile_send, speed, potential_temp, wind_field, eddy_diff,
            district[:, owned + 16 : owned + 32, :], before, after,
        ),
    )
    (temp_next,) = call(
        deposit_body,
        [VMEM] * 6,
        [sds(potential_temp.shape, F32)],
        (returned, pick, air, coef, cells, base),
        [pltpu.VMEM((slots, 128), F32), pltpu.VMEM((128, 64), F32)],
        flops=2 * 64 * 128 * slots * 128,
    )
    return temp_next, wall_next


def solution(mesh):
    in_specs = (
        P("gz", "xy", None),
        P(None, "gz", "xy", None),
        P("gz", "xy", None),
        P("gz", "xy", None),
        P("gz", "xy"),
        P("gz", "xy"),
        P("gz", "xy", None, None),
        P("gz", "xy"),
        P(),
        P("xy", "gz", None, None),
        P("xy", None, "gz"),
    )
    out_specs = (P("gz", "xy", None), P("gz", "xy", None, None))
    return jax.shard_map(
        on_device, mesh=mesh, in_specs=in_specs, out_specs=out_specs, check_vma=False
    )
```

```python
import functools

import jax
import jax.numpy as jnp
from jax import lax
from jax.experimental import pallas as pl
from jax.experimental.pallas import tpu as pltpu
from jax.sharding import PartitionSpec as P


wall_gain = 0.25
flux_gain = 0.5
FULL = 60 << 20

F32 = jnp.float32
BF16 = jnp.bfloat16
VMEM = pl.BlockSpec(memory_space=pltpu.VMEM)
HBM = pl.BlockSpec(memory_space=pltpu.HBM)
SMEM = pl.BlockSpec(memory_space=pltpu.SMEM)


def sds(shape, dtype):
    return jax.ShapeDtypeStruct(shape, dtype)


def call(body, in_specs, outs, args, scratch=(), flops=0, nbytes=1 << 20, limit=12 << 20, out_specs=None):
    return pl.pallas_call(
        body,
        in_specs=in_specs,
        out_specs=out_specs or tuple(VMEM for _ in outs),
        out_shape=tuple(outs),
        scratch_shapes=list(scratch),
        compiler_params=pltpu.CompilerParams(vmem_limit_bytes=limit),
        cost_estimate=pl.CostEstimate(flops=flops, bytes_accessed=nbytes, transcendentals=0),
    )(*args)


def iota(shape, dim):
    return lax.broadcasted_iota(jnp.int32, shape, dim)


def dot(lhs, rhs, dims=((1,), (0,))):
    return lax.dot_general(lhs, rhs, (dims, ((), ())), preferred_element_type=F32)


def column(row, size):
    picked = jnp.where(iota((size, size), 0) == iota((size, size), 1), row, 0.0)
    return jnp.sum(picked, axis=1, keepdims=True)


def split(value):
    high = value.astype(BF16)
    return high, (value - high.astype(F32)).astype(BF16)


def pack_body(wall_ref, pair_ref, theta_ref, out_ref, node_ref, near_ref, level_ref, ids_ref, plane_ref, sems):
    copies = [
        pltpu.make_async_copy(wall_ref.at[0, :, 0, :], node_ref, sems.at[0]),
        pltpu.make_async_copy(pair_ref, near_ref, sems.at[1]),
        pltpu.make_async_copy(theta_ref, level_ref, sems.at[2]),
    ]
    for copy in copies:
        copy.start()
    level = lax.axis_index("gz")
    parts = out_ref.shape[0]
    owned = node_ref.shape[0]
    ids_ref[...] = jnp.full(ids_ref.shape, -1.0, F32)
    for copy in copies:
        copy.wait()
    target = near_ref[0, 0:1, :]
    blocks = target.shape[1]
    for side in range(2):
        for q in range(4):
            plane_ref[side, 4 * q : 4 * q + 4, :] = level_ref[side, :, 128 * q : 128 * q + 128]
    emitted = node_ref[...].astype(BF16)
    for dest in range(parts):
        near = target - dest * owned
        inside = (near >= 0) & (near < owned)
        ids_ref[0:1, 0:blocks] = jnp.where(inside, near, -1).astype(F32)
        up = jnp.where(level + 1 == dest, plane_ref[1], 0.0)
        down = jnp.where(level - 1 == dest, plane_ref[0], 0.0)
        out_ref[dest, 0:owned, :] = emitted
        out_ref[dest, owned : owned + 16, :] = ids_ref[...].astype(BF16)
        out_ref[dest, owned + 16 : owned + 32, :] = (up + down).astype(BF16)


def lookup_body(theta_ref, wind_ref, cell_ref, send_ref, air_ref, speed_ref, out_ref, theta_tab, speed_tab):
    theta = jnp.concatenate([theta_ref[0], theta_ref[1]], axis=0)
    speed = jnp.zeros_like(theta)
    for d in range(3):
        w = jnp.concatenate([wind_ref[d, 0], wind_ref[d, 1]], axis=0)
        speed = speed + w * w
    for q in range(4):
        theta_tab[8 * q : 8 * q + 8, :] = theta[:, 128 * q : 128 * q + 128]
        speed_tab[8 * q : 8 * q + 8, :] = 4.0 * speed[:, 128 * q : 128 * q + 128]
    slots = cell_ref.shape[0]

    def group(p, carry):
        base = pl.multiple_of(p * 8, 8)
        cells = cell_ref[pl.ds(base, 8), :]
        lane = cells & 127
        line = ((cells >> 7) & 3) * 8 + (cells >> 9)
        air = jnp.zeros((8, 128), F32)
        spd = jnp.zeros((8, 128), F32)
        for r in range(32):
            here = line == r
            for_air = jnp.broadcast_to(theta_tab[r : r + 1, :], (8, 128))
            for_spd = jnp.broadcast_to(speed_tab[r : r + 1, :], (8, 128))
            for_air = jnp.take_along_axis(for_air, lane, axis=1, mode="promise_in_bounds")
            for_spd = jnp.take_along_axis(for_spd, lane, axis=1, mode="promise_in_bounds")
            air = jnp.where(here, for_air, air)
            spd = jnp.where(here, for_spd, spd)
        air_ref[pl.ds(base, 8), :] = air
        speed_ref[pl.ds(base, 8), :] = spd
        return carry

    lax.fori_loop(0, slots // 8, group, 0, unroll=8)
    owners = slots // 2
    wanted = iota((slots, slots), 0)
    wanted = jnp.where(wanted < owners, 2 * wanted, 2 * (wanted - owners) + 1)
    hit = jnp.where(send_ref[...] == wanted, 1.0, 0.0).astype(BF16)
    both = jnp.concatenate([air_ref[...].astype(BF16), speed_ref[...].astype(BF16)], axis=1)
    both = dot(hit, both)
    for place in range(2):
        out_ref[place] = both[place * owners : (place + 1) * owners, :128]
        out_ref[2 + place] = both[place * owners : (place + 1) * owners, 128:]


def reflect_body(pair_ref, recv_ref, block_ref, out_ref, add_ref, all_ref, src_ref):
    parts, owned, blocks = recv_ref.shape[0], add_ref.shape[0], block_ref.shape[1]
    lane = iota((1, 128), 1)
    ids = jnp.zeros((1, 128), F32)
    for part in range(parts):
        all_ref[part * owned : (part + 1) * owned, :] = recv_ref[part, 0:owned, :].astype(F32)
        row = recv_ref[part, owned : owned + 16, :].astype(F32)[0:1, :]
        row = jnp.where(lane < blocks, row, 0.0)
        ids = ids + (pltpu.roll(row, part * blocks, 1) if part else row)
    for b in range(blocks):
        src_ref[b : b + 1, :] = all_ref[pl.ds(pair_ref[0, 1, b], 1), :]
    source = src_ref[...].astype(BF16)
    which = iota((blocks, 128), 0)
    total = jnp.zeros((blocks, 128), F32)
    for b in range(blocks):
        one = dot(source, block_ref[0, b], ((1,), (1,)))
        total = jnp.where(which == b, one, total)
    for part in range(parts):
        out_ref[part] = total.astype(BF16)
    hot = iota(add_ref.shape, 0).astype(F32) == ids
    add_ref[...] = jnp.where(hot, 1.0, 0.0).astype(BF16)


def cubics(g1, g2, g3, g4):
    first = (g4, -(2.0 * g1 * g3 + g2 * g2), 3.0 * g1 * g1 * g2, -(g1 * g1) * (g1 * g1))
    second = (g3, -2.0 * g1 * g2, g1 * g1 * g1)
    third = (g2, -(g1 * g1))
    return first, second, third, (g1,)


def weighted(curves, rows):
    totals = []
    for power in range(4):
        terms = [curve[power] if row is None else curve[power] * row
                 for curve, row in zip(curves, rows) if power < len(curve)]
        totals.append(functools.reduce(lambda x, y: x + y, terms))
    return totals


def wall_body(
    class_ref, inverse_ref, wall_ref, take_ref,
    free_ref, rows_ref, gain_ref, resp_ref, lam_ref, mix_ref, table_ref, take_out, back_out, kind_ref, lhs_ref,
):
    nodes = inverse_ref.shape[1]
    full = functools.partial(
        lax.dot_general,
        dimension_numbers=(((1,), (0,)), ((), ())),
        precision=lax.Precision.HIGHEST,
        preferred_element_type=F32,
    )
    for c in range(inverse_ref.shape[0]):
        one = inverse_ref[c]
        two = full(one, one)
        three = full(two, one)
        four = full(two, two)
        stack = jnp.concatenate(
            [four, one[0:1], two[0:1], three[0:1], jnp.zeros((13, nodes), F32)], axis=0
        )
        high, low = split(stack)
        lhs_ref[c] = jnp.concatenate([high, high, low], axis=1)
        for k, power in enumerate((one, two, three, four)):
            resp_ref[c, k] = jnp.broadcast_to(power[:, 0:1], (nodes, 128))
        curves = cubics(*[resp_ref[c, k, 0:1, :] for k in range(4)])
        for power, value in enumerate(weighted(curves, [None] * 4)):
            table_ref[4 * c + power : 4 * c + power + 1, :] = value

    owned = wall_ref.shape[1]

    def tiles(g, carry):
        base = pl.multiple_of(g * 8, 8)
        firsts = [[], [], [], [], []]
        gains = [[], [], [], []]
        kinds = []
        for q in range(8):
            t = base + q
            kind = class_ref[0, t]
            kinds.append(jnp.full((1, 128), kind, jnp.int32))
            state = wall_ref[0, t]
            high, low = split(state)
            result = dot(lhs_ref[kind], jnp.concatenate([high, low, high], axis=0))
            free_ref[t] = result[0:nodes]
            for k in range(3):
                firsts[k].append(result[nodes + k : nodes + k + 1])
            firsts[3].append(state[0:1])
            firsts[4].append(result[0:1])
            for k in range(4):
                gains[k].append(resp_ref[kind, k, 0:1, :])
        for k in range(5):
            rows_ref[k, pl.ds(base, 8), :] = jnp.concatenate(firsts[k], axis=0)
        for k in range(4):
            gain_ref[k, pl.ds(base, 8), :] = jnp.concatenate(gains[k], axis=0)
        kind_ref[pl.ds(base, 8), :] = jnp.concatenate(kinds, axis=0).astype(F32)
        return carry

    lax.fori_loop(0, owned // 8, tiles, 0, unroll=2)
    curves = cubics(gain_ref[0], gain_ref[1], gain_ref[2], gain_ref[3])
    for power, value in enumerate(weighted(curves, [None] * 4)):
        lam_ref[power] = value
    before = [rows_ref[3], rows_ref[0], rows_ref[1], rows_ref[2]]
    for power, value in enumerate(weighted(curves, before)):
        mix_ref[power] = value
    take = take_ref[...]
    col = column(take.astype(F32), owned).astype(jnp.int32)
    lanes = iota((owned, 2 * owned), 1)
    place = (col & 1) * owned + (col >> 1)
    take_out[...] = jnp.where(lanes == place, 1.0, 0.0).astype(BF16)
    wanted = iota((2 * owned, owned), 0)
    wanted = jnp.where(wanted < owned, 2 * wanted, 2 * (wanted - owned) + 1)
    back_out[...] = jnp.where(take == wanted, 1.0, 0.0).astype(BF16)


def blend_body(refl_ref, add_ref, rows_ref, lam_ref, mix_ref, kind_ref, back_ref, fwd_ref, out_ref, rad_ref, list_ref):
    parts, blocks = refl_ref.shape[0], refl_ref.shape[1]
    owned = add_ref.shape[0]
    rad = dot(add_ref[...], refl_ref[...].reshape(parts * blocks, 128))
    rad_ref[...] = rad
    quarter = wall_gain * rad
    poly = [rows_ref[4] + quarter * lam_ref[0]]
    for power in range(1, 4):
        poly.append(quarter * lam_ref[power] - mix_ref[power - 1])
    poly += [-mix_ref[3], kind_ref[...]]
    placed = dot(back_ref[...], jnp.concatenate([p.astype(BF16) for p in poly], axis=1))
    for t in range(4):
        list_ref[pl.ds(t, owned, stride=16), :] = fwd_ref[t]
    for place in range(2):
        for m in range(6):
            value = placed[place * owned : (place + 1) * owned, 128 * m : 128 * m + 128]
            list_ref[pl.ds(4 + 6 * place + m, owned, stride=16), :] = value
    out_ref[...] = list_ref[...].astype(BF16)


def upwind(speed, centre, lower, upper):
    return jnp.maximum(speed, 0.0) * (centre - lower) + jnp.minimum(speed, 0.0) * (upper - centre)


def air_body(
    theta_ref, wind_ref, eddy_ref, zhalo_ref, before_ref, after_ref, send_ref, speed_ref, base_ref, pick_ref, coef_ref
):
    slots = send_ref.shape[1]
    col = column(send_ref[...].astype(F32), slots)
    live = col >= 0.0
    whole = col.astype(jnp.int32)
    place = jnp.where(live, (whole & 1) * (slots // 2) + (whole >> 1), -1)
    pick_ref[...] = jnp.where(iota((slots, slots), 1) == place, 1.0, 0.0).astype(BF16)
    coef_ref[...] = jnp.where(live, 0.5 + speed_ref[...], 0.0)
    level = lax.axis_index("gz")
    parts = zhalo_ref.shape[0]

    def plane(from_part, valid):
        value = zhalo_ref[jnp.clip(from_part, 0, parts - 1)].astype(F32)
        value = jnp.concatenate([value[4 * q : 4 * q + 4] for q in range(4)], axis=1)
        return jnp.where(valid, value, 0.0)

    below = plane(level - 1, level > 0)
    above = plane(level + 1, level < parts - 1)
    for k in range(2):
        c = theta_ref[k]
        lower_z = theta_ref[0] if k else below
        upper_z = above if k else theta_ref[1]
        lower_x = jnp.concatenate([before_ref[k], c[0:3]], axis=0)
        upper_x = jnp.concatenate([c[1:4], after_ref[k]], axis=0)
        lower_y = jnp.concatenate([c[:, -1:], c[:, :-1]], axis=1)
        upper_y = jnp.concatenate([c[:, 1:], c[:, :1]], axis=1)
        advect = (
            upwind(wind_ref[0, k], c, lower_z, upper_z)
            + upwind(wind_ref[1, k], c, lower_x, upper_x)
            + upwind(wind_ref[2, k], c, lower_y, upper_y)
        )
        laplace = lower_z + upper_z + lower_x + upper_x + lower_y + upper_y - 6.0 * c
        base_ref[k] = c - advect + eddy_ref[k] * laplace


def close_body(
    class_ref, recv_ref, take_ref, rows_ref, gain_ref, rad_ref, free_ref, resp_ref,
    pick_ref, air_ref, coef_ref, table_ref, cell_ref, base_ref,
    wall_hbm, out_ref, list_ref, force_ref, wall_ref, flux_ref, acc_ref, sem,
):
    list_ref[...] = recv_ref[...].astype(F32)
    owned = rad_ref.shape[0]

    def part(t):
        return list_ref[pl.ds(t, owned, stride=16), :].astype(BF16)

    taken = jnp.concatenate(
        [jnp.concatenate([part(0), part(1)], axis=0), jnp.concatenate([part(2), part(3)], axis=0)], axis=1
    )
    taken = dot(take_ref[...], taken)
    air = taken[:, :128]
    quarter = wall_gain * (0.5 + taken[:, 128:])
    rad = wall_gain * rad_ref[...]
    g1, g2, g3 = gain_ref[0], gain_ref[1], gain_ref[2]
    f0 = quarter * (air - rows_ref[3]) + rad
    f1 = quarter * (air - (rows_ref[0] + g1 * f0)) + rad
    f2 = quarter * (air - (rows_ref[1] + (g2 * f0 + g1 * f1))) + rad
    f3 = quarter * (air - (rows_ref[2] + (g3 * f0 + g2 * f1 + g1 * f2))) + rad
    force_ref[0] = f0
    force_ref[1] = f1
    force_ref[2] = f2
    force_ref[3] = f3

    def tile(t, carry):
        kind = class_ref[0, t]
        value = free_ref[t]
        for k in range(4):
            value = value + resp_ref[kind, 3 - k] * force_ref[k, pl.ds(t, 1), :]
        wall_ref[0, t] = value
        return carry

    lax.fori_loop(0, owned, tile, 0, unroll=4)
    copy = pltpu.make_async_copy(wall_ref, wall_hbm, sem)
    copy.start()

    slots = cell_ref.shape[0]
    back = [jnp.concatenate([part(4 + m), part(10 + m)], axis=0) for m in range(6)]
    back = dot(pick_ref[...], jnp.concatenate(back, axis=1))
    poly = [back[:, 128 * m : 128 * m + 128] for m in range(6)]
    own_air, own_coef = air_ref[...], coef_ref[...]
    h = wall_gain * own_coef
    lam = jnp.zeros((slots, 128), F32)
    for c in range(table_ref.shape[0] // 4):
        one = [table_ref[4 * c + power : 4 * c + power + 1, :] for power in range(4)]
        lam = jnp.where(poly[5] == float(c), one[0] + h * (one[1] + h * (one[2] + h * one[3])), lam)
    surface = poly[0] + h * (poly[1] + h * (poly[2] + h * (poly[3] + h * poly[4]))) + h * own_air * lam
    flux_ref[...] = own_coef * (surface - own_air)
    count = 8
    lanes = iota((128, count * 128), 0).astype(BF16)
    lines = iota((32, count * 128), 0).astype(BF16)
    acc_ref[...] = jnp.zeros_like(acc_ref)

    def flat(rows):
        return jnp.concatenate([rows[i : i + 1] for i in range(count)], axis=1)

    def group(p, carry):
        base = pl.multiple_of(p * count, count)
        cells = cell_ref[pl.ds(base, count), :]
        lane = flat((cells & 127).astype(F32)).astype(BF16)
        line = flat((((cells >> 7) & 3) * 8 + (cells >> 9)).astype(F32)).astype(BF16)
        high, low = split(flat(flux_ref[pl.ds(base, count), :]))
        hot = jnp.where(lanes == lane, BF16(1), BF16(0))
        here = lines == line
        placed = jnp.concatenate([jnp.where(here, high, BF16(0)), jnp.where(here, low, BF16(0))], axis=0)
        acc_ref[...] += dot(hot, placed, ((1,), (1,)))
        return carry

    lax.fori_loop(0, slots // count, group, 0, unroll=8)
    heat = acc_ref[...].T
    heat = heat[0:32] + heat[32:64]
    heat = jnp.concatenate([heat[8 * q : 8 * q + 8] for q in range(4)], axis=1)
    for k in range(2):
        out_ref[k] = base_ref[k] + flux_gain * heat[4 * k : 4 * k + 4]
    copy.wait()


def on_device(
    potential_temp,
    wind_field,
    eddy_diff,
    facade_cell,
    tile_send,
    tile_take,
    wall_temp,
    wall_class,
    wall_inverse,
    refl_block,
    refl_pair,
):
    slots = facade_cell.shape[1]
    owned = tile_take.shape[1]
    nodes = wall_temp.shape[2]
    classes = wall_inverse.shape[0]
    blocks = refl_block.shape[1]
    parts = lax.axis_size("gz")
    xy_count = lax.axis_size("xy")
    cells = facade_cell.reshape(slots, 128)
    dma = pltpu.SemaphoreType.DMA

    (payload,) = call(
        pack_body,
        [HBM] * 3,
        [sds((parts, owned + 32, 128), BF16)],
        (wall_temp, refl_pair, potential_temp),
        [
            pltpu.VMEM((owned, 128), F32),
            pltpu.VMEM(refl_pair.shape, jnp.int32),
            pltpu.VMEM(potential_temp.shape, F32),
            pltpu.VMEM((16, 128), F32),
            pltpu.VMEM((2, 16, 128), F32),
            dma((3,)),
        ],
        limit=FULL,
    )
    district = lax.all_to_all(payload, "gz", split_axis=0, concat_axis=0, tiled=True)

    air, speed, forward = call(
        lookup_body,
        [VMEM] * 4,
        [sds((slots, 128), F32), sds((slots, 128), F32), sds((4, slots // 2, 128), F32)],
        (potential_temp, wind_field, cells, tile_send),
        [pltpu.VMEM((32, 128), F32), pltpu.VMEM((32, 128), F32)],
        flops=2 * 48 * 256 * slots * 128,
    )
    row4 = sds((4, owned, 128), F32)
    free, rows, gain, resp, lam, mix, table, take_pick, back_pick, kind = call(
        wall_body,
        [SMEM] + [VMEM] * 3,
        [
            sds((owned, nodes, 128), F32),
            sds((5, owned, 128), F32),
            row4,
            sds((classes, 4, nodes, 128), F32),
            row4,
            row4,
            sds((4 * classes, 128), F32),
            sds((owned, 2 * owned), BF16),
            sds((2 * owned, owned), BF16),
            sds((owned, 128), F32),
        ],
        (wall_class, wall_inverse, wall_temp, tile_take),
        [pltpu.VMEM((classes, nodes + 16, 3 * nodes), BF16)],
        flops=2 * 48 * 96 * owned * 128,
    )
    district, forward, mix = lax.optimization_barrier((district, forward, mix))
    contrib, add_matrix = call(
        reflect_body,
        [SMEM, VMEM, VMEM],
        [sds((parts, blocks, 128), BF16), sds((owned, 128), BF16)],
        (refl_pair, district, refl_block),
        [pltpu.VMEM((parts * owned, 128), F32), pltpu.VMEM((blocks, 128), F32)],
    )
    reflected = lax.all_to_all(contrib, "gz", split_axis=0, concat_axis=0, tiled=True)

    last = xy_count - 1
    before = lax.ppermute(potential_temp[:, 3:4, :], "xy", [(i, i + 1) for i in range(last)])
    after = lax.ppermute(potential_temp[:, 0:1, :], "xy", [(i + 1, i) for i in range(last)])

    send_list, rad = call(
        blend_body,
        [VMEM] * 8,
        [sds((16 * xy_count, 128), BF16), sds((owned, 128), F32)],
        (reflected, add_matrix, rows, lam, mix, kind, back_pick, forward),
        [pltpu.VMEM((16 * xy_count, 128), F32)],
    )
    received = lax.all_to_all(send_list, "xy", split_axis=0, concat_axis=0, tiled=True)
    base, pick, coef = call(
        air_body,
        [VMEM] * 8,
        [sds(potential_temp.shape, F32), sds((slots, slots), BF16), sds((slots, 128), F32)],
        (
            potential_temp, wind_field, eddy_diff, district[:, owned + 16 : owned + 32, :], before, after,
            tile_send, speed,
        ),
    )
    wall_next, temp_next = call(
        close_body,
        [SMEM] + [VMEM] * 13,
        [sds((1, owned, nodes, 128), F32), sds(potential_temp.shape, F32)],
        (
            wall_class, received, take_pick, rows, gain, rad, free, resp,
            pick, air, coef, table, cells, base,
        ),
        [
            pltpu.VMEM((16 * xy_count, 128), F32),
            pltpu.VMEM((4, owned, 128), F32),
            pltpu.VMEM((1, owned, nodes, 128), F32),
            pltpu.VMEM((slots, 128), F32),
            pltpu.VMEM((128, 64), F32),
            dma,
        ],
        flops=2 * 64 * 128 * slots * 128,
        out_specs=(pl.BlockSpec(memory_space=pl.ANY), VMEM),
    )
    return temp_next, wall_next


def solution(mesh):
    in_specs = (
        P("gz", "xy", None),
        P(None, "gz", "xy", None),
        P("gz", "xy", None),
        P("gz", "xy", None),
        P("gz", "xy"),
        P("gz", "xy"),
        P("gz", "xy", None, None),
        P("gz", "xy"),
        P(),
        P("xy", "gz", None, None),
        P("xy", None, "gz"),
    )
    out_specs = (P("gz", "xy", None), P("gz", "xy", None, None))
    return jax.shard_map(on_device, mesh=mesh, in_specs=in_specs, out_specs=out_specs, check_vma=False)
```

```python
import functools

import jax
import jax.numpy as jnp
from jax import lax
from jax.experimental import pallas as pl
from jax.experimental.pallas import tpu as pltpu
from jax.sharding import PartitionSpec as P


wall_gain = 0.25
flux_gain = 0.5
FULL = 60 << 20

F32 = jnp.float32
BF16 = jnp.bfloat16
VMEM = pl.BlockSpec(memory_space=pltpu.VMEM)
HBM = pl.BlockSpec(memory_space=pltpu.HBM)
SMEM = pl.BlockSpec(memory_space=pltpu.SMEM)


def sds(shape, dtype):
    return jax.ShapeDtypeStruct(shape, dtype)


def call(body, in_specs, outs, args, scratch=(), flops=0, nbytes=1 << 20, limit=12 << 20, out_specs=None):
    return pl.pallas_call(
        body,
        in_specs=in_specs,
        out_specs=out_specs or tuple(VMEM for _ in outs),
        out_shape=tuple(outs),
        scratch_shapes=list(scratch),
        compiler_params=pltpu.CompilerParams(vmem_limit_bytes=limit),
        cost_estimate=pl.CostEstimate(flops=flops, bytes_accessed=nbytes, transcendentals=0),
    )(*args)


def iota(shape, dim):
    return lax.broadcasted_iota(jnp.int32, shape, dim)


def dot(lhs, rhs, dims=((1,), (0,))):
    return lax.dot_general(lhs, rhs, (dims, ((), ())), preferred_element_type=F32)


def column(row, size):
    picked = jnp.where(iota((size, size), 0) == iota((size, size), 1), row, 0.0)
    return jnp.sum(picked, axis=1, keepdims=True)


def split(value):
    high = value.astype(BF16)
    return high, (value - high.astype(F32)).astype(BF16)


def pack_body(wall_ref, pair_ref, theta_ref, out_ref, node_ref, near_ref, level_ref, ids_ref, plane_ref, sems):
    copies = [
        pltpu.make_async_copy(wall_ref.at[0, :, 0, :], node_ref, sems.at[0]),
        pltpu.make_async_copy(pair_ref, near_ref, sems.at[1]),
        pltpu.make_async_copy(theta_ref, level_ref, sems.at[2]),
    ]
    for copy in copies:
        copy.start()
    level = lax.axis_index("gz")
    parts = out_ref.shape[0]
    owned = node_ref.shape[0]
    ids_ref[...] = jnp.full(ids_ref.shape, -1.0, F32)
    for copy in copies:
        copy.wait()
    target = near_ref[0, 0:1, :]
    blocks = target.shape[1]
    for side in range(2):
        for q in range(4):
            plane_ref[side, 4 * q : 4 * q + 4, :] = level_ref[side, :, 128 * q : 128 * q + 128]
    emitted = node_ref[...].astype(BF16)
    for dest in range(parts):
        near = target - dest * owned
        inside = (near >= 0) & (near < owned)
        ids_ref[0:1, 0:blocks] = jnp.where(inside, near, -1).astype(F32)
        up = jnp.where(level + 1 == dest, plane_ref[1], 0.0)
        down = jnp.where(level - 1 == dest, plane_ref[0], 0.0)
        out_ref[dest, 0:owned, :] = emitted
        out_ref[dest, owned : owned + 16, :] = ids_ref[...].astype(BF16)
        out_ref[dest, owned + 16 : owned + 32, :] = (up + down).astype(BF16)


def lookup_body(
    theta_ref, wind_ref, cell_ref, send_ref, pair_ref,
    air_ref, speed_ref, out_ref, pair_out, theta_tab, speed_tab,
):
    pair_out[...] = pair_ref[...]
    theta = jnp.concatenate([theta_ref[0], theta_ref[1]], axis=0)
    speed = jnp.zeros_like(theta)
    for d in range(3):
        w = jnp.concatenate([wind_ref[d, 0], wind_ref[d, 1]], axis=0)
        speed = speed + w * w
    for q in range(4):
        theta_tab[8 * q : 8 * q + 8, :] = theta[:, 128 * q : 128 * q + 128]
        speed_tab[8 * q : 8 * q + 8, :] = 4.0 * speed[:, 128 * q : 128 * q + 128]
    slots = cell_ref.shape[0]

    def group(p, carry):
        base = pl.multiple_of(p * 8, 8)
        cells = cell_ref[pl.ds(base, 8), :]
        lane = cells & 127
        line = ((cells >> 7) & 3) * 8 + (cells >> 9)
        air = jnp.zeros((8, 128), F32)
        spd = jnp.zeros((8, 128), F32)
        for r in range(32):
            here = line == r
            for_air = jnp.broadcast_to(theta_tab[r : r + 1, :], (8, 128))
            for_spd = jnp.broadcast_to(speed_tab[r : r + 1, :], (8, 128))
            for_air = jnp.take_along_axis(for_air, lane, axis=1, mode="promise_in_bounds")
            for_spd = jnp.take_along_axis(for_spd, lane, axis=1, mode="promise_in_bounds")
            air = jnp.where(here, for_air, air)
            spd = jnp.where(here, for_spd, spd)
        air_ref[pl.ds(base, 8), :] = air
        speed_ref[pl.ds(base, 8), :] = spd
        return carry

    lax.fori_loop(0, slots // 8, group, 0, unroll=8)
    owners = slots // 2
    wanted = iota((slots, slots), 0)
    wanted = jnp.where(wanted < owners, 2 * wanted, 2 * (wanted - owners) + 1)
    hit = jnp.where(send_ref[...] == wanted, 1.0, 0.0).astype(BF16)
    both = jnp.concatenate([air_ref[...].astype(BF16), speed_ref[...].astype(BF16)], axis=1)
    both = dot(hit, both)
    for place in range(2):
        out_ref[place] = both[place * owners : (place + 1) * owners, :128]
        out_ref[2 + place] = both[place * owners : (place + 1) * owners, 128:]


def reflect_body(pair_ref, recv_ref, block_ref, out_ref, add_ref, all_ref, src_ref):
    parts, owned, blocks = recv_ref.shape[0], add_ref.shape[0], block_ref.shape[1]
    lane = iota((1, 128), 1)
    ids = jnp.zeros((1, 128), F32)
    for part in range(parts):
        all_ref[part * owned : (part + 1) * owned, :] = recv_ref[part, 0:owned, :].astype(F32)
        row = recv_ref[part, owned : owned + 16, :].astype(F32)[0:1, :]
        row = jnp.where(lane < blocks, row, 0.0)
        ids = ids + (pltpu.roll(row, part * blocks, 1) if part else row)
    for b in range(blocks):
        src_ref[b : b + 1, :] = all_ref[pl.ds(pair_ref[0, 1, b], 1), :]
    source = src_ref[...].astype(BF16)
    which = iota((blocks, 128), 0)
    total = jnp.zeros((blocks, 128), F32)
    for b in range(blocks):
        one = dot(source, block_ref[0, b], ((1,), (1,)))
        total = jnp.where(which == b, one, total)
    for part in range(parts):
        out_ref[part] = total.astype(BF16)
    hot = iota(add_ref.shape, 0).astype(F32) == ids
    add_ref[...] = jnp.where(hot, 1.0, 0.0).astype(BF16)


def cubics(g1, g2, g3, g4):
    first = (g4, -(2.0 * g1 * g3 + g2 * g2), 3.0 * g1 * g1 * g2, -(g1 * g1) * (g1 * g1))
    second = (g3, -2.0 * g1 * g2, g1 * g1 * g1)
    third = (g2, -(g1 * g1))
    return first, second, third, (g1,)


def weighted(curves, rows):
    totals = []
    for power in range(4):
        terms = [curve[power] if row is None else curve[power] * row
                 for curve, row in zip(curves, rows) if power < len(curve)]
        totals.append(functools.reduce(lambda x, y: x + y, terms))
    return totals


def wall_body(
    class_ref, inverse_ref, wall_ref, take_ref,
    free_ref, rows_ref, gain_ref, resp_ref, lam_ref, mix_ref, table_ref, take_out, back_out, kind_ref, lhs_ref,
):
    nodes = inverse_ref.shape[1]
    full = functools.partial(
        lax.dot_general,
        dimension_numbers=(((1,), (0,)), ((), ())),
        precision=lax.Precision.HIGHEST,
        preferred_element_type=F32,
    )
    for c in range(inverse_ref.shape[0]):
        one = inverse_ref[c]
        two = full(one, one)
        three = full(two, one)
        four = full(two, two)
        stack = jnp.concatenate(
            [four, one[0:1], two[0:1], three[0:1], jnp.zeros((13, nodes), F32)], axis=0
        )
        high, low = split(stack)
        lhs_ref[c] = jnp.concatenate([high, high, low], axis=1)
        for k, power in enumerate((one, two, three, four)):
            resp_ref[c, k] = jnp.broadcast_to(power[:, 0:1], (nodes, 128))
        curves = cubics(*[resp_ref[c, k, 0:1, :] for k in range(4)])
        for power, value in enumerate(weighted(curves, [None] * 4)):
            table_ref[4 * c + power : 4 * c + power + 1, :] = value

    owned = wall_ref.shape[1]

    def tiles(g, carry):
        base = pl.multiple_of(g * 8, 8)
        firsts = [[], [], [], [], []]
        gains = [[], [], [], []]
        kinds = []
        for q in range(8):
            t = base + q
            kind = class_ref[0, t]
            kinds.append(jnp.full((1, 128), kind, jnp.int32))
            state = wall_ref[0, t]
            high, low = split(state)
            result = dot(lhs_ref[kind], jnp.concatenate([high, low, high], axis=0))
            free_ref[t] = result[0:nodes]
            for k in range(3):
                firsts[k].append(result[nodes + k : nodes + k + 1])
            firsts[3].append(state[0:1])
            firsts[4].append(result[0:1])
            for k in range(4):
                gains[k].append(resp_ref[kind, k, 0:1, :])
        for k in range(5):
            rows_ref[k, pl.ds(base, 8), :] = jnp.concatenate(firsts[k], axis=0)
        for k in range(4):
            gain_ref[k, pl.ds(base, 8), :] = jnp.concatenate(gains[k], axis=0)
        kind_ref[pl.ds(base, 8), :] = jnp.concatenate(kinds, axis=0).astype(F32)
        return carry

    lax.fori_loop(0, owned // 8, tiles, 0, unroll=2)
    curves = cubics(gain_ref[0], gain_ref[1], gain_ref[2], gain_ref[3])
    for power, value in enumerate(weighted(curves, [None] * 4)):
        lam_ref[power] = value
    before = [rows_ref[3], rows_ref[0], rows_ref[1], rows_ref[2]]
    for power, value in enumerate(weighted(curves, before)):
        mix_ref[power] = value
    take = take_ref[...]
    col = column(take.astype(F32), owned).astype(jnp.int32)
    lanes = iota((owned, 2 * owned), 1)
    place = (col & 1) * owned + (col >> 1)
    take_out[...] = jnp.where(lanes == place, 1.0, 0.0).astype(BF16)
    wanted = iota((2 * owned, owned), 0)
    wanted = jnp.where(wanted < owned, 2 * wanted, 2 * (wanted - owned) + 1)
    back_out[...] = jnp.where(take == wanted, 1.0, 0.0).astype(BF16)


def blend_body(refl_ref, add_ref, rows_ref, lam_ref, mix_ref, kind_ref, back_ref, fwd_ref, out_ref, rad_ref, list_ref):
    parts, blocks = refl_ref.shape[0], refl_ref.shape[1]
    owned = add_ref.shape[0]
    rad = dot(add_ref[...], refl_ref[...].reshape(parts * blocks, 128))
    rad_ref[...] = rad
    quarter = wall_gain * rad
    poly = [rows_ref[4] + quarter * lam_ref[0]]
    for power in range(1, 4):
        poly.append(quarter * lam_ref[power] - mix_ref[power - 1])
    poly += [-mix_ref[3], kind_ref[...]]
    placed = dot(back_ref[...], jnp.concatenate([p.astype(BF16) for p in poly], axis=1))
    for t in range(4):
        list_ref[pl.ds(t, owned, stride=16), :] = fwd_ref[t]
    for place in range(2):
        for m in range(6):
            value = placed[place * owned : (place + 1) * owned, 128 * m : 128 * m + 128]
            list_ref[pl.ds(4 + 6 * place + m, owned, stride=16), :] = value
    out_ref[...] = list_ref[...].astype(BF16)


def upwind(speed, centre, lower, upper):
    return jnp.maximum(speed, 0.0) * (centre - lower) + jnp.minimum(speed, 0.0) * (upper - centre)


def air_body(
    theta_ref, wind_ref, eddy_ref, zhalo_ref, before_ref, after_ref, send_ref, speed_ref, base_ref, pick_ref, coef_ref
):
    slots = send_ref.shape[1]
    col = column(send_ref[...].astype(F32), slots)
    live = col >= 0.0
    whole = col.astype(jnp.int32)
    place = jnp.where(live, (whole & 1) * (slots // 2) + (whole >> 1), -1)
    pick_ref[...] = jnp.where(iota((slots, slots), 1) == place, 1.0, 0.0).astype(BF16)
    coef_ref[...] = jnp.where(live, 0.5 + speed_ref[...], 0.0)
    level = lax.axis_index("gz")
    parts = zhalo_ref.shape[0]

    def plane(from_part, valid):
        value = zhalo_ref[jnp.clip(from_part, 0, parts - 1)].astype(F32)
        value = jnp.concatenate([value[4 * q : 4 * q + 4] for q in range(4)], axis=1)
        return jnp.where(valid, value, 0.0)

    below = plane(level - 1, level > 0)
    above = plane(level + 1, level < parts - 1)
    for k in range(2):
        c = theta_ref[k]
        lower_z = theta_ref[0] if k else below
        upper_z = above if k else theta_ref[1]
        lower_x = jnp.concatenate([before_ref[k], c[0:3]], axis=0)
        upper_x = jnp.concatenate([c[1:4], after_ref[k]], axis=0)
        lower_y = jnp.concatenate([c[:, -1:], c[:, :-1]], axis=1)
        upper_y = jnp.concatenate([c[:, 1:], c[:, :1]], axis=1)
        advect = (
            upwind(wind_ref[0, k], c, lower_z, upper_z)
            + upwind(wind_ref[1, k], c, lower_x, upper_x)
            + upwind(wind_ref[2, k], c, lower_y, upper_y)
        )
        laplace = lower_z + upper_z + lower_x + upper_x + lower_y + upper_y - 6.0 * c
        base_ref[k] = c - advect + eddy_ref[k] * laplace


def close_body(
    class_ref, recv_ref, take_ref, rows_ref, gain_ref, rad_ref, free_ref, resp_ref,
    pick_ref, air_ref, coef_ref, table_ref, cell_ref, base_ref,
    wall_hbm, out_ref, list_ref, force_ref, wall_ref, flux_ref, acc_ref, sem,
):
    list_ref[...] = recv_ref[...].astype(F32)
    owned = rad_ref.shape[0]

    def part(t):
        return list_ref[pl.ds(t, owned, stride=16), :].astype(BF16)

    taken = jnp.concatenate(
        [jnp.concatenate([part(0), part(1)], axis=0), jnp.concatenate([part(2), part(3)], axis=0)], axis=1
    )
    taken = dot(take_ref[...], taken)
    air = taken[:, :128]
    quarter = wall_gain * (0.5 + taken[:, 128:])
    rad = wall_gain * rad_ref[...]
    g1, g2, g3 = gain_ref[0], gain_ref[1], gain_ref[2]
    f0 = quarter * (air - rows_ref[3]) + rad
    f1 = quarter * (air - (rows_ref[0] + g1 * f0)) + rad
    f2 = quarter * (air - (rows_ref[1] + (g2 * f0 + g1 * f1))) + rad
    f3 = quarter * (air - (rows_ref[2] + (g3 * f0 + g2 * f1 + g1 * f2))) + rad
    force_ref[0] = f0
    force_ref[1] = f1
    force_ref[2] = f2
    force_ref[3] = f3

    def tile(t, carry):
        kind = class_ref[0, t]
        value = free_ref[t]
        for k in range(4):
            value = value + resp_ref[kind, 3 - k] * force_ref[k, pl.ds(t, 1), :]
        wall_ref[0, t] = value
        return carry

    lax.fori_loop(0, owned, tile, 0, unroll=8)
    copy = pltpu.make_async_copy(wall_ref, wall_hbm, sem)
    copy.start()

    slots = cell_ref.shape[0]
    back = [jnp.concatenate([part(4 + m), part(10 + m)], axis=0) for m in range(6)]
    back = dot(pick_ref[...], jnp.concatenate(back, axis=1))
    poly = [back[:, 128 * m : 128 * m + 128] for m in range(6)]
    own_air, own_coef = air_ref[...], coef_ref[...]
    h = wall_gain * own_coef
    lam = jnp.zeros((slots, 128), F32)
    for c in range(table_ref.shape[0] // 4):
        one = [table_ref[4 * c + power : 4 * c + power + 1, :] for power in range(4)]
        lam = jnp.where(poly[5] == float(c), one[0] + h * (one[1] + h * (one[2] + h * one[3])), lam)
    surface = poly[0] + h * (poly[1] + h * (poly[2] + h * (poly[3] + h * poly[4]))) + h * own_air * lam
    flux_ref[...] = own_coef * (surface - own_air)
    count = 8
    lanes = iota((128, count * 128), 0).astype(BF16)
    lines = iota((32, count * 128), 0).astype(BF16)
    acc_ref[...] = jnp.zeros_like(acc_ref)

    def flat(rows):
        return jnp.concatenate([rows[i : i + 1] for i in range(count)], axis=1)

    def group(p, carry):
        base = pl.multiple_of(p * count, count)
        cells = cell_ref[pl.ds(base, count), :]
        lane = flat((cells & 127).astype(F32)).astype(BF16)
        line = flat((((cells >> 7) & 3) * 8 + (cells >> 9)).astype(F32)).astype(BF16)
        high, low = split(flat(flux_ref[pl.ds(base, count), :]))
        hot = jnp.where(lanes == lane, BF16(1), BF16(0))
        here = lines == line
        placed = jnp.concatenate([jnp.where(here, high, BF16(0)), jnp.where(here, low, BF16(0))], axis=0)
        acc_ref[...] += dot(hot, placed, ((1,), (1,)))
        return carry

    lax.fori_loop(0, slots // count, group, 0, unroll=16)
    heat = acc_ref[...].T
    heat = heat[0:32] + heat[32:64]
    heat = jnp.concatenate([heat[8 * q : 8 * q + 8] for q in range(4)], axis=1)
    for k in range(2):
        out_ref[k] = base_ref[k] + flux_gain * heat[4 * k : 4 * k + 4]
    copy.wait()


def on_device(
    potential_temp,
    wind_field,
    eddy_diff,
    facade_cell,
    tile_send,
    tile_take,
    wall_temp,
    wall_class,
    wall_inverse,
    refl_block,
    refl_pair,
):
    slots = facade_cell.shape[1]
    owned = tile_take.shape[1]
    nodes = wall_temp.shape[2]
    classes = wall_inverse.shape[0]
    blocks = refl_block.shape[1]
    parts = lax.axis_size("gz")
    xy_count = lax.axis_size("xy")
    cells = facade_cell.reshape(slots, 128)
    dma = pltpu.SemaphoreType.DMA

    (payload,) = call(
        pack_body,
        [HBM] * 3,
        [sds((parts, owned + 32, 128), BF16)],
        (wall_temp, refl_pair, potential_temp),
        [
            pltpu.VMEM((owned, 128), F32),
            pltpu.VMEM(refl_pair.shape, jnp.int32),
            pltpu.VMEM(potential_temp.shape, F32),
            pltpu.VMEM((16, 128), F32),
            pltpu.VMEM((2, 16, 128), F32),
            dma((3,)),
        ],
        limit=FULL,
    )
    district = lax.all_to_all(payload, "gz", split_axis=0, concat_axis=0, tiled=True)

    air, speed, forward, pair = call(
        lookup_body,
        [VMEM] * 5,
        [
            sds((slots, 128), F32),
            sds((slots, 128), F32),
            sds((4, slots // 2, 128), F32),
            sds(refl_pair.shape, jnp.int32),
        ],
        (potential_temp, wind_field, cells, tile_send, refl_pair),
        [pltpu.VMEM((32, 128), F32), pltpu.VMEM((32, 128), F32)],
        flops=2 * 48 * 256 * slots * 128,
    )
    row4 = sds((4, owned, 128), F32)
    free, rows, gain, resp, lam, mix, table, take_pick, back_pick, kind = call(
        wall_body,
        [SMEM] + [VMEM] * 3,
        [
            sds((owned, nodes, 128), F32),
            sds((5, owned, 128), F32),
            row4,
            sds((classes, 4, nodes, 128), F32),
            row4,
            row4,
            sds((4 * classes, 128), F32),
            sds((owned, 2 * owned), BF16),
            sds((2 * owned, owned), BF16),
            sds((owned, 128), F32),
        ],
        (wall_class, wall_inverse, wall_temp, tile_take),
        [pltpu.VMEM((classes, nodes + 16, 3 * nodes), BF16)],
        flops=2 * 48 * 96 * owned * 128,
    )
    district, forward, mix = lax.optimization_barrier((district, forward, mix))
    contrib, add_matrix = call(
        reflect_body,
        [SMEM, VMEM, VMEM],
        [sds((parts, blocks, 128), BF16), sds((owned, 128), BF16)],
        (pair, district, refl_block),
        [pltpu.VMEM((parts * owned, 128), F32), pltpu.VMEM((blocks, 128), F32)],
    )
    reflected = lax.all_to_all(contrib, "gz", split_axis=0, concat_axis=0, tiled=True)

    last = xy_count - 1
    before = lax.ppermute(potential_temp[:, 3:4, :], "xy", [(i, i + 1) for i in range(last)])
    after = lax.ppermute(potential_temp[:, 0:1, :], "xy", [(i + 1, i) for i in range(last)])

    send_list, rad = call(
        blend_body,
        [VMEM] * 8,
        [sds((16 * xy_count, 128), BF16), sds((owned, 128), F32)],
        (reflected, add_matrix, rows, lam, mix, kind, back_pick, forward),
        [pltpu.VMEM((16 * xy_count, 128), F32)],
    )
    received = lax.all_to_all(send_list, "xy", split_axis=0, concat_axis=0, tiled=True)
    base, pick, coef = call(
        air_body,
        [VMEM] * 8,
        [sds(potential_temp.shape, F32), sds((slots, slots), BF16), sds((slots, 128), F32)],
        (
            potential_temp, wind_field, eddy_diff, district[:, owned + 16 : owned + 32, :], before, after,
            tile_send, speed,
        ),
    )
    wall_next, temp_next = call(
        close_body,
        [SMEM] + [VMEM] * 13,
        [sds((1, owned, nodes, 128), F32), sds(potential_temp.shape, F32)],
        (
            wall_class, received, take_pick, rows, gain, rad, free, resp,
            pick, air, coef, table, cells, base,
        ),
        [
            pltpu.VMEM((16 * xy_count, 128), F32),
            pltpu.VMEM((4, owned, 128), F32),
            pltpu.VMEM((1, owned, nodes, 128), F32),
            pltpu.VMEM((slots, 128), F32),
            pltpu.VMEM((128, 64), F32),
            dma,
        ],
        flops=2 * 64 * 128 * slots * 128,
        out_specs=(pl.BlockSpec(memory_space=pl.ANY), VMEM),
    )
    return temp_next, wall_next


def solution(mesh):
    in_specs = (
        P("gz", "xy", None),
        P(None, "gz", "xy", None),
        P("gz", "xy", None),
        P("gz", "xy", None),
        P("gz", "xy"),
        P("gz", "xy"),
        P("gz", "xy", None, None),
        P("gz", "xy"),
        P(),
        P("xy", "gz", None, None),
        P("xy", None, "gz"),
    )
    out_specs = (P("gz", "xy", None), P("gz", "xy", None, None))
    return jax.shard_map(
        on_device, mesh=mesh, in_specs=in_specs, out_specs=out_specs, check_vma=False
    )
```

```python
import functools

import jax
import jax.numpy as jnp
from jax import lax
from jax.experimental import pallas as pl
from jax.experimental.pallas import tpu as pltpu
from jax.sharding import PartitionSpec as P


wall_gain = 0.25
flux_gain = 0.5
FULL = 60 << 20

F32 = jnp.float32
BF16 = jnp.bfloat16
VMEM = pl.BlockSpec(memory_space=pltpu.VMEM)
HBM = pl.BlockSpec(memory_space=pltpu.HBM)
SMEM = pl.BlockSpec(memory_space=pltpu.SMEM)


def sds(shape, dtype):
    return jax.ShapeDtypeStruct(shape, dtype)


def call(body, in_specs, outs, args, scratch=(), flops=0, nbytes=1 << 20, limit=12 << 20, out_specs=None):
    return pl.pallas_call(
        body,
        in_specs=in_specs,
        out_specs=out_specs or tuple(VMEM for _ in outs),
        out_shape=tuple(outs),
        scratch_shapes=list(scratch),
        compiler_params=pltpu.CompilerParams(vmem_limit_bytes=limit),
        cost_estimate=pl.CostEstimate(flops=flops, bytes_accessed=nbytes, transcendentals=0),
    )(*args)


def iota(shape, dim):
    return lax.broadcasted_iota(jnp.int32, shape, dim)


def dot(lhs, rhs, dims=((1,), (0,))):
    return lax.dot_general(lhs, rhs, (dims, ((), ())), preferred_element_type=F32)


def column(row, size):
    picked = jnp.where(iota((size, size), 0) == iota((size, size), 1), row, 0.0)
    return jnp.sum(picked, axis=1, keepdims=True)


def split(value):
    high = value.astype(BF16)
    return high, (value - high.astype(F32)).astype(BF16)


def pack_body(wall_ref, pair_ref, theta_ref, out_ref, node_ref, near_ref, level_ref, ids_ref, plane_ref, sems):
    copies = [
        pltpu.make_async_copy(wall_ref.at[0, :, 0, :], node_ref, sems.at[0]),
        pltpu.make_async_copy(pair_ref, near_ref, sems.at[1]),
        pltpu.make_async_copy(theta_ref, level_ref, sems.at[2]),
    ]
    for copy in copies:
        copy.start()
    level = lax.axis_index("gz")
    parts = out_ref.shape[0]
    owned = node_ref.shape[0]
    ids_ref[...] = jnp.full(ids_ref.shape, -1.0, F32)
    for copy in copies:
        copy.wait()
    target = near_ref[0, 0:1, :]
    blocks = target.shape[1]
    for side in range(2):
        for q in range(4):
            plane_ref[side, 4 * q : 4 * q + 4, :] = level_ref[side, :, 128 * q : 128 * q + 128]
    emitted = node_ref[...].astype(BF16)
    for dest in range(parts):
        near = target - dest * owned
        inside = (near >= 0) & (near < owned)
        ids_ref[0:1, 0:blocks] = jnp.where(inside, near, -1).astype(F32)
        up = jnp.where(level + 1 == dest, plane_ref[1], 0.0)
        down = jnp.where(level - 1 == dest, plane_ref[0], 0.0)
        out_ref[dest, 0:owned, :] = emitted
        out_ref[dest, owned : owned + 16, :] = ids_ref[...].astype(BF16)
        out_ref[dest, owned + 16 : owned + 32, :] = (up + down).astype(BF16)


def lookup_body(
    theta_ref, wind_ref, cell_ref, send_ref, pair_ref,
    air_ref, speed_ref, out_ref, pair_out, theta_tab, speed_tab,
):
    pair_out[...] = pair_ref[...]
    theta = jnp.concatenate([theta_ref[0], theta_ref[1]], axis=0)
    speed = jnp.zeros_like(theta)
    for d in range(3):
        w = jnp.concatenate([wind_ref[d, 0], wind_ref[d, 1]], axis=0)
        speed = speed + w * w
    for q in range(4):
        theta_tab[8 * q : 8 * q + 8, :] = theta[:, 128 * q : 128 * q + 128]
        speed_tab[8 * q : 8 * q + 8, :] = 4.0 * speed[:, 128 * q : 128 * q + 128]
    slots = cell_ref.shape[0]

    def group(p, carry):
        base = pl.multiple_of(p * 8, 8)
        cells = cell_ref[pl.ds(base, 8), :]
        lane = cells & 127
        line = ((cells >> 7) & 3) * 8 + (cells >> 9)
        air = jnp.zeros((8, 128), F32)
        spd = jnp.zeros((8, 128), F32)
        for r in range(32):
            here = line == r
            for_air = jnp.broadcast_to(theta_tab[r : r + 1, :], (8, 128))
            for_spd = jnp.broadcast_to(speed_tab[r : r + 1, :], (8, 128))
            for_air = jnp.take_along_axis(for_air, lane, axis=1, mode="promise_in_bounds")
            for_spd = jnp.take_along_axis(for_spd, lane, axis=1, mode="promise_in_bounds")
            air = jnp.where(here, for_air, air)
            spd = jnp.where(here, for_spd, spd)
        air_ref[pl.ds(base, 8), :] = air
        speed_ref[pl.ds(base, 8), :] = spd
        return carry

    lax.fori_loop(0, slots // 8, group, 0, unroll=8)
    owners = slots // 2
    wanted = iota((slots, slots), 0)
    wanted = jnp.where(wanted < owners, 2 * wanted, 2 * (wanted - owners) + 1)
    hit = jnp.where(send_ref[...] == wanted, 1.0, 0.0).astype(BF16)
    both = jnp.concatenate([air_ref[...].astype(BF16), speed_ref[...].astype(BF16)], axis=1)
    both = dot(hit, both)
    for place in range(2):
        out_ref[place] = both[place * owners : (place + 1) * owners, :128]
        out_ref[2 + place] = both[place * owners : (place + 1) * owners, 128:]


def reflect_body(pair_ref, recv_ref, block_ref, out_ref, add_ref, all_ref, src_ref):
    parts, owned, blocks = recv_ref.shape[0], add_ref.shape[0], block_ref.shape[1]
    lane = iota((1, 128), 1)
    ids = jnp.zeros((1, 128), F32)
    for part in range(parts):
        all_ref[part * owned : (part + 1) * owned, :] = recv_ref[part, 0:owned, :].astype(F32)
        row = recv_ref[part, owned : owned + 16, :].astype(F32)[0:1, :]
        row = jnp.where(lane < blocks, row, 0.0)
        ids = ids + (pltpu.roll(row, part * blocks, 1) if part else row)
    for b in range(blocks):
        src_ref[b : b + 1, :] = all_ref[pl.ds(pair_ref[0, 1, b], 1), :]
    source = src_ref[...].astype(BF16)
    which = iota((blocks, 128), 0)
    total = jnp.zeros((blocks, 128), F32)
    for b in range(blocks):
        one = dot(source, block_ref[0, b], ((1,), (1,)))
        total = jnp.where(which == b, one, total)
    for part in range(parts):
        out_ref[part] = total.astype(BF16)
    hot = iota(add_ref.shape, 0).astype(F32) == ids
    add_ref[...] = jnp.where(hot, 1.0, 0.0).astype(BF16)


def cubics(g1, g2, g3, g4):
    first = (g4, -(2.0 * g1 * g3 + g2 * g2), 3.0 * g1 * g1 * g2, -(g1 * g1) * (g1 * g1))
    second = (g3, -2.0 * g1 * g2, g1 * g1 * g1)
    third = (g2, -(g1 * g1))
    return first, second, third, (g1,)


def weighted(curves, rows):
    totals = []
    for power in range(4):
        terms = [curve[power] if row is None else curve[power] * row
                 for curve, row in zip(curves, rows) if power < len(curve)]
        totals.append(functools.reduce(lambda x, y: x + y, terms))
    return totals


def wall_body(
    class_ref, inverse_ref, wall_ref, take_ref,
    free_ref, rows_ref, gain_ref, resp_ref, lam_ref, mix_ref, table_ref, take_out, back_out, kind_ref, lhs_ref,
):
    nodes = inverse_ref.shape[1]
    full = functools.partial(
        lax.dot_general,
        dimension_numbers=(((1,), (0,)), ((), ())),
        precision=lax.Precision.HIGHEST,
        preferred_element_type=F32,
    )
    for c in range(inverse_ref.shape[0]):
        one = inverse_ref[c]
        two = full(one, one)
        three = full(two, one)
        four = full(two, two)
        stack = jnp.concatenate(
            [four, one[0:1], two[0:1], three[0:1], jnp.zeros((13, nodes), F32)], axis=0
        )
        high, low = split(stack)
        lhs_ref[c] = jnp.concatenate([high, high, low], axis=1)
        for k, power in enumerate((one, two, three, four)):
            resp_ref[c, k] = jnp.broadcast_to(power[:, 0:1], (nodes, 128))
        curves = cubics(*[resp_ref[c, k, 0:1, :] for k in range(4)])
        for power, value in enumerate(weighted(curves, [None] * 4)):
            table_ref[4 * c + power : 4 * c + power + 1, :] = value

    owned = wall_ref.shape[1]

    def tiles(g, carry):
        base = pl.multiple_of(g * 8, 8)
        firsts = [[], [], [], [], []]
        gains = [[], [], [], []]
        kinds = []
        for q in range(8):
            t = base + q
            kind = class_ref[0, t]
            kinds.append(jnp.full((1, 128), kind, jnp.int32))
            state = wall_ref[0, t]
            high, low = split(state)
            result = dot(lhs_ref[kind], jnp.concatenate([high, low, high], axis=0))
            free_ref[t] = result[0:nodes]
            for k in range(3):
                firsts[k].append(result[nodes + k : nodes + k + 1])
            firsts[3].append(state[0:1])
            firsts[4].append(result[0:1])
            for k in range(4):
                gains[k].append(resp_ref[kind, k, 0:1, :])
        for k in range(5):
            rows_ref[k, pl.ds(base, 8), :] = jnp.concatenate(firsts[k], axis=0)
        for k in range(4):
            gain_ref[k, pl.ds(base, 8), :] = jnp.concatenate(gains[k], axis=0)
        kind_ref[pl.ds(base, 8), :] = jnp.concatenate(kinds, axis=0).astype(F32)
        return carry

    lax.fori_loop(0, owned // 8, tiles, 0, unroll=2)
    curves = cubics(gain_ref[0], gain_ref[1], gain_ref[2], gain_ref[3])
    for power, value in enumerate(weighted(curves, [None] * 4)):
        lam_ref[power] = value
    before = [rows_ref[3], rows_ref[0], rows_ref[1], rows_ref[2]]
    for power, value in enumerate(weighted(curves, before)):
        mix_ref[power] = value
    take = take_ref[...]
    col = column(take.astype(F32), owned).astype(jnp.int32)
    lanes = iota((owned, 2 * owned), 1)
    place = (col & 1) * owned + (col >> 1)
    take_out[...] = jnp.where(lanes == place, 1.0, 0.0).astype(BF16)
    wanted = iota((2 * owned, owned), 0)
    wanted = jnp.where(wanted < owned, 2 * wanted, 2 * (wanted - owned) + 1)
    back_out[...] = jnp.where(take == wanted, 1.0, 0.0).astype(BF16)


def blend_body(refl_ref, add_ref, rows_ref, lam_ref, mix_ref, kind_ref, back_ref, fwd_ref, out_ref, rad_ref, list_ref):
    parts, blocks = refl_ref.shape[0], refl_ref.shape[1]
    owned = add_ref.shape[0]
    rad = dot(add_ref[...], refl_ref[...].reshape(parts * blocks, 128))
    rad_ref[...] = rad
    quarter = wall_gain * rad
    poly = [rows_ref[4] + quarter * lam_ref[0]]
    for power in range(1, 4):
        poly.append(quarter * lam_ref[power] - mix_ref[power - 1])
    poly += [-mix_ref[3], kind_ref[...]]
    placed = dot(back_ref[...], jnp.concatenate([p.astype(BF16) for p in poly], axis=1))
    for t in range(4):
        list_ref[pl.ds(t, owned, stride=16), :] = fwd_ref[t]
    for place in range(2):
        for m in range(6):
            value = placed[place * owned : (place + 1) * owned, 128 * m : 128 * m + 128]
            list_ref[pl.ds(4 + 6 * place + m, owned, stride=16), :] = value
    out_ref[...] = list_ref[...].astype(BF16)


def upwind(speed, centre, lower, upper):
    return jnp.maximum(speed, 0.0) * (centre - lower) + jnp.minimum(speed, 0.0) * (upper - centre)


def air_body(
    theta_ref, wind_ref, eddy_ref, zhalo_ref, near_ref, far_ref, send_ref, speed_ref, base_ref, pick_ref, coef_ref
):
    slots = send_ref.shape[1]
    col = column(send_ref[...].astype(F32), slots)
    live = col >= 0.0
    whole = col.astype(jnp.int32)
    place = jnp.where(live, (whole & 1) * (slots // 2) + (whole >> 1), -1)
    pick_ref[...] = jnp.where(iota((slots, slots), 1) == place, 1.0, 0.0).astype(BF16)
    coef_ref[...] = jnp.where(live, 0.5 + speed_ref[...], 0.0)
    level = lax.axis_index("gz")
    parts = zhalo_ref.shape[0]

    def plane(from_part, valid):
        value = zhalo_ref[jnp.clip(from_part, 0, parts - 1)].astype(F32)
        value = jnp.concatenate([value[4 * q : 4 * q + 4] for q in range(4)], axis=1)
        return jnp.where(valid, value, 0.0)

    below = plane(level - 1, level > 0)
    above = plane(level + 1, level < parts - 1)
    even = lax.axis_index("xy") % 2 == 0
    for k in range(2):
        before = jnp.where(even, far_ref[k], near_ref[k])
        after = jnp.where(even, near_ref[k], far_ref[k])
        c = theta_ref[k]
        lower_z = theta_ref[0] if k else below
        upper_z = above if k else theta_ref[1]
        lower_x = jnp.concatenate([before, c[0:3]], axis=0)
        upper_x = jnp.concatenate([c[1:4], after], axis=0)
        lower_y = jnp.concatenate([c[:, -1:], c[:, :-1]], axis=1)
        upper_y = jnp.concatenate([c[:, 1:], c[:, :1]], axis=1)
        advect = (
            upwind(wind_ref[0, k], c, lower_z, upper_z)
            + upwind(wind_ref[1, k], c, lower_x, upper_x)
            + upwind(wind_ref[2, k], c, lower_y, upper_y)
        )
        laplace = lower_z + upper_z + lower_x + upper_x + lower_y + upper_y - 6.0 * c
        base_ref[k] = c - advect + eddy_ref[k] * laplace


def close_body(
    class_ref, recv_ref, take_ref, rows_ref, gain_ref, rad_ref, free_ref, resp_ref,
    pick_ref, air_ref, coef_ref, table_ref, cell_ref, base_ref,
    wall_hbm, out_ref, list_ref, force_ref, wall_ref, flux_ref, acc_ref, sem,
):
    list_ref[...] = recv_ref[...].astype(F32)
    owned = rad_ref.shape[0]

    def part(t):
        return list_ref[pl.ds(t, owned, stride=16), :].astype(BF16)

    taken = jnp.concatenate(
        [jnp.concatenate([part(0), part(1)], axis=0), jnp.concatenate([part(2), part(3)], axis=0)], axis=1
    )
    taken = dot(take_ref[...], taken)
    air = taken[:, :128]
    quarter = wall_gain * (0.5 + taken[:, 128:])
    rad = wall_gain * rad_ref[...]
    g1, g2, g3 = gain_ref[0], gain_ref[1], gain_ref[2]
    f0 = quarter * (air - rows_ref[3]) + rad
    f1 = quarter * (air - (rows_ref[0] + g1 * f0)) + rad
    f2 = quarter * (air - (rows_ref[1] + (g2 * f0 + g1 * f1))) + rad
    f3 = quarter * (air - (rows_ref[2] + (g3 * f0 + g2 * f1 + g1 * f2))) + rad
    force_ref[0] = f0
    force_ref[1] = f1
    force_ref[2] = f2
    force_ref[3] = f3

    def tile(t, carry):
        kind = class_ref[0, t]
        value = free_ref[t]
        for k in range(4):
            value = value + resp_ref[kind, 3 - k] * force_ref[k, pl.ds(t, 1), :]
        wall_ref[0, t] = value
        return carry

    lax.fori_loop(0, owned, tile, 0, unroll=4)
    copy = pltpu.make_async_copy(wall_ref, wall_hbm, sem)
    copy.start()

    slots = cell_ref.shape[0]
    back = [jnp.concatenate([part(4 + m), part(10 + m)], axis=0) for m in range(6)]
    back = dot(pick_ref[...], jnp.concatenate(back, axis=1))
    poly = [back[:, 128 * m : 128 * m + 128] for m in range(6)]
    own_air, own_coef = air_ref[...], coef_ref[...]
    h = wall_gain * own_coef
    lam = jnp.zeros((slots, 128), F32)
    for c in range(table_ref.shape[0] // 4):
        one = [table_ref[4 * c + power : 4 * c + power + 1, :] for power in range(4)]
        lam = jnp.where(poly[5] == float(c), one[0] + h * (one[1] + h * (one[2] + h * one[3])), lam)
    surface = poly[0] + h * (poly[1] + h * (poly[2] + h * (poly[3] + h * poly[4]))) + h * own_air * lam
    flux_ref[...] = own_coef * (surface - own_air)
    count = 8
    lanes = iota((128, count * 128), 0).astype(BF16)
    lines = iota((32, count * 128), 0).astype(BF16)
    acc_ref[...] = jnp.zeros_like(acc_ref)

    def flat(rows):
        return jnp.concatenate([rows[i : i + 1] for i in range(count)], axis=1)

    def group(p, carry):
        base = pl.multiple_of(p * count, count)
        cells = cell_ref[pl.ds(base, count), :]
        lane = flat((cells & 127).astype(F32)).astype(BF16)
        line = flat((((cells >> 7) & 3) * 8 + (cells >> 9)).astype(F32)).astype(BF16)
        high, low = split(flat(flux_ref[pl.ds(base, count), :]))
        hot = jnp.where(lanes == lane, BF16(1), BF16(0))
        here = lines == line
        placed = jnp.concatenate([jnp.where(here, high, BF16(0)), jnp.where(here, low, BF16(0))], axis=0)
        acc_ref[...] += dot(hot, placed, ((1,), (1,)))
        return carry

    lax.fori_loop(0, slots // count, group, 0, unroll=8)
    heat = acc_ref[...].T
    heat = heat[0:32] + heat[32:64]
    heat = jnp.concatenate([heat[8 * q : 8 * q + 8] for q in range(4)], axis=1)
    for k in range(2):
        out_ref[k] = base_ref[k] + flux_gain * heat[4 * k : 4 * k + 4]
    copy.wait()


def on_device(
    potential_temp,
    wind_field,
    eddy_diff,
    facade_cell,
    tile_send,
    tile_take,
    wall_temp,
    wall_class,
    wall_inverse,
    refl_block,
    refl_pair,
):
    slots = facade_cell.shape[1]
    owned = tile_take.shape[1]
    nodes = wall_temp.shape[2]
    classes = wall_inverse.shape[0]
    blocks = refl_block.shape[1]
    parts = lax.axis_size("gz")
    xy_count = lax.axis_size("xy")
    cells = facade_cell.reshape(slots, 128)
    dma = pltpu.SemaphoreType.DMA

    (payload,) = call(
        pack_body,
        [HBM] * 3,
        [sds((parts, owned + 32, 128), BF16)],
        (wall_temp, refl_pair, potential_temp),
        [
            pltpu.VMEM((owned, 128), F32),
            pltpu.VMEM(refl_pair.shape, jnp.int32),
            pltpu.VMEM(potential_temp.shape, F32),
            pltpu.VMEM((16, 128), F32),
            pltpu.VMEM((2, 16, 128), F32),
            dma((3,)),
        ],
        limit=FULL,
    )
    district = lax.all_to_all(payload, "gz", split_axis=0, concat_axis=0, tiled=True)

    air, speed, forward, pair = call(
        lookup_body,
        [VMEM] * 5,
        [
            sds((slots, 128), F32),
            sds((slots, 128), F32),
            sds((4, slots // 2, 128), F32),
            sds(refl_pair.shape, jnp.int32),
        ],
        (potential_temp, wind_field, cells, tile_send, refl_pair),
        [pltpu.VMEM((32, 128), F32), pltpu.VMEM((32, 128), F32)],
        flops=2 * 48 * 256 * slots * 128,
    )
    row4 = sds((4, owned, 128), F32)
    free, rows, gain, resp, lam, mix, table, take_pick, back_pick, kind = call(
        wall_body,
        [SMEM] + [VMEM] * 3,
        [
            sds((owned, nodes, 128), F32),
            sds((5, owned, 128), F32),
            row4,
            sds((classes, 4, nodes, 128), F32),
            row4,
            row4,
            sds((4 * classes, 128), F32),
            sds((owned, 2 * owned), BF16),
            sds((2 * owned, owned), BF16),
            sds((owned, 128), F32),
        ],
        (wall_class, wall_inverse, wall_temp, tile_take),
        [pltpu.VMEM((classes, nodes + 16, 3 * nodes), BF16)],
        flops=2 * 48 * 96 * owned * 128,
    )
    district, forward, mix = lax.optimization_barrier((district, forward, mix))
    contrib, add_matrix = call(
        reflect_body,
        [SMEM, VMEM, VMEM],
        [sds((parts, blocks, 128), BF16), sds((owned, 128), BF16)],
        (pair, district, refl_block),
        [pltpu.VMEM((parts * owned, 128), F32), pltpu.VMEM((blocks, 128), F32)],
    )
    reflected = lax.all_to_all(contrib, "gz", split_axis=0, concat_axis=0, tiled=True)

    even = lax.axis_index("xy") % 2 == 0
    first_row, last_row = potential_temp[:, 0:1, :], potential_temp[:, 3:4, :]
    mates = [(i, i + 1) for i in range(0, xy_count, 2)]
    others = [(i, i + 1) for i in range(1, xy_count - 1, 2)]
    near = lax.ppermute(jnp.where(even, last_row, first_row), "xy", mates + [(j, i) for i, j in mates])
    far = lax.ppermute(jnp.where(even, first_row, last_row), "xy", others + [(j, i) for i, j in others])

    send_list, rad = call(
        blend_body,
        [VMEM] * 8,
        [sds((16 * xy_count, 128), BF16), sds((owned, 128), F32)],
        (reflected, add_matrix, rows, lam, mix, kind, back_pick, forward),
        [pltpu.VMEM((16 * xy_count, 128), F32)],
    )
    received = lax.all_to_all(send_list, "xy", split_axis=0, concat_axis=0, tiled=True)
    base, pick, coef = call(
        air_body,
        [VMEM] * 8,
        [sds(potential_temp.shape, F32), sds((slots, slots), BF16), sds((slots, 128), F32)],
        (
            potential_temp, wind_field, eddy_diff, district[:, owned + 16 : owned + 32, :], near, far,
            tile_send, speed,
        ),
    )
    wall_next, temp_next = call(
        close_body,
        [SMEM] + [VMEM] * 13,
        [sds((1, owned, nodes, 128), F32), sds(potential_temp.shape, F32)],
        (
            wall_class, received, take_pick, rows, gain, rad, free, resp,
            pick, air, coef, table, cells, base,
        ),
        [
            pltpu.VMEM((16 * xy_count, 128), F32),
            pltpu.VMEM((4, owned, 128), F32),
            pltpu.VMEM((1, owned, nodes, 128), F32),
            pltpu.VMEM((slots, 128), F32),
            pltpu.VMEM((128, 64), F32),
            dma,
        ],
        flops=2 * 64 * 128 * slots * 128,
        out_specs=(pl.BlockSpec(memory_space=pl.ANY), VMEM),
    )
    return temp_next, wall_next


def solution(mesh):
    in_specs = (
        P("gz", "xy", None),
        P(None, "gz", "xy", None),
        P("gz", "xy", None),
        P("gz", "xy", None),
        P("gz", "xy"),
        P("gz", "xy"),
        P("gz", "xy", None, None),
        P("gz", "xy"),
        P(),
        P("xy", "gz", None, None),
        P("xy", None, "gz"),
    )
    out_specs = (P("gz", "xy", None), P("gz", "xy", None, None))
    return jax.shard_map(on_device, mesh=mesh, in_specs=in_specs, out_specs=out_specs, check_vma=False)
```

```python
import functools

import jax
import jax.numpy as jnp
from jax import lax
from jax.experimental import pallas as pl
from jax.experimental.pallas import tpu as pltpu
from jax.sharding import PartitionSpec as P


wall_gain = 0.25
flux_gain = 0.5
FULL = 60 << 20

F32 = jnp.float32
BF16 = jnp.bfloat16
VMEM = pl.BlockSpec(memory_space=pltpu.VMEM)
HBM = pl.BlockSpec(memory_space=pltpu.HBM)
SMEM = pl.BlockSpec(memory_space=pltpu.SMEM)


def sds(shape, dtype):
    return jax.ShapeDtypeStruct(shape, dtype)


def call(body, in_specs, outs, args, scratch=(), flops=0, nbytes=1 << 20, limit=12 << 20, out_specs=None):
    return pl.pallas_call(
        body,
        in_specs=in_specs,
        out_specs=out_specs or tuple(VMEM for _ in outs),
        out_shape=tuple(outs),
        scratch_shapes=list(scratch),
        compiler_params=pltpu.CompilerParams(vmem_limit_bytes=limit),
        cost_estimate=pl.CostEstimate(flops=flops, bytes_accessed=nbytes, transcendentals=0),
    )(*args)


def iota(shape, dim):
    return lax.broadcasted_iota(jnp.int32, shape, dim)


def dot(lhs, rhs, dims=((1,), (0,))):
    return lax.dot_general(lhs, rhs, (dims, ((), ())), preferred_element_type=F32)


def column(row, size):
    picked = jnp.where(iota((size, size), 0) == iota((size, size), 1), row, 0.0)
    return jnp.sum(picked, axis=1, keepdims=True)


def split(value):
    high = value.astype(BF16)
    return high, (value - high.astype(F32)).astype(BF16)


def pack_body(wall_ref, pair_ref, theta_ref, out_ref, node_ref, near_ref, level_ref, ids_ref, plane_ref, sems):
    copies = [
        pltpu.make_async_copy(wall_ref.at[0, :, 0, :], node_ref, sems.at[0]),
        pltpu.make_async_copy(pair_ref, near_ref, sems.at[1]),
        pltpu.make_async_copy(theta_ref, level_ref, sems.at[2]),
    ]
    for copy in copies:
        copy.start()
    level = lax.axis_index("gz")
    parts = out_ref.shape[0]
    owned = node_ref.shape[0]
    ids_ref[...] = jnp.full(ids_ref.shape, -1.0, F32)
    for copy in copies:
        copy.wait()
    target = near_ref[0, 0:1, :]
    blocks = target.shape[1]
    for side in range(2):
        for q in range(4):
            plane_ref[side, 4 * q : 4 * q + 4, :] = level_ref[side, :, 128 * q : 128 * q + 128]
    emitted = node_ref[...].astype(BF16)
    for dest in range(parts):
        near = target - dest * owned
        inside = (near >= 0) & (near < owned)
        ids_ref[0:1, 0:blocks] = jnp.where(inside, near, -1).astype(F32)
        up = jnp.where(level + 1 == dest, plane_ref[1], 0.0)
        down = jnp.where(level - 1 == dest, plane_ref[0], 0.0)
        out_ref[dest, 0:owned, :] = emitted
        out_ref[dest, owned : owned + 8, :] = ids_ref[...].astype(BF16)
        out_ref[dest, owned + 8 : owned + 24, :] = (up + down).astype(BF16)


def lookup_body(
    theta_ref, wind_ref, cell_ref, send_ref, pair_ref,
    air_ref, speed_ref, out_ref, pair_out, theta_tab, speed_tab,
):
    pair_out[...] = pair_ref[...]
    theta = jnp.concatenate([theta_ref[0], theta_ref[1]], axis=0)
    speed = jnp.zeros_like(theta)
    for d in range(3):
        w = jnp.concatenate([wind_ref[d, 0], wind_ref[d, 1]], axis=0)
        speed = speed + w * w
    for q in range(4):
        theta_tab[8 * q : 8 * q + 8, :] = theta[:, 128 * q : 128 * q + 128]
        speed_tab[8 * q : 8 * q + 8, :] = 4.0 * speed[:, 128 * q : 128 * q + 128]
    slots = cell_ref.shape[0]

    def group(p, carry):
        base = pl.multiple_of(p * 8, 8)
        cells = cell_ref[pl.ds(base, 8), :]
        lane = cells & 127
        line = ((cells >> 7) & 3) * 8 + (cells >> 9)
        air = jnp.zeros((8, 128), F32)
        spd = jnp.zeros((8, 128), F32)
        for r in range(32):
            here = line == r
            for_air = jnp.broadcast_to(theta_tab[r : r + 1, :], (8, 128))
            for_spd = jnp.broadcast_to(speed_tab[r : r + 1, :], (8, 128))
            for_air = jnp.take_along_axis(for_air, lane, axis=1, mode="promise_in_bounds")
            for_spd = jnp.take_along_axis(for_spd, lane, axis=1, mode="promise_in_bounds")
            air = jnp.where(here, for_air, air)
            spd = jnp.where(here, for_spd, spd)
        air_ref[pl.ds(base, 8), :] = air
        speed_ref[pl.ds(base, 8), :] = spd
        return carry

    lax.fori_loop(0, slots // 8, group, 0, unroll=8)
    owners = slots // 2
    wanted = iota((slots, slots), 0)
    wanted = jnp.where(wanted < owners, 2 * wanted, 2 * (wanted - owners) + 1)
    hit = jnp.where(send_ref[...] == wanted, 1.0, 0.0).astype(BF16)
    both = jnp.concatenate([air_ref[...].astype(BF16), speed_ref[...].astype(BF16)], axis=1)
    both = dot(hit, both)
    for place in range(2):
        out_ref[place] = both[place * owners : (place + 1) * owners, :128]
        out_ref[2 + place] = both[place * owners : (place + 1) * owners, 128:]


def reflect_body(pair_ref, recv_ref, block_ref, out_ref, add_ref, all_ref, src_ref):
    parts, owned, blocks = recv_ref.shape[0], add_ref.shape[0], block_ref.shape[1]
    lane = iota((1, 128), 1)
    ids = jnp.zeros((1, 128), F32)
    for part in range(parts):
        all_ref[part * owned : (part + 1) * owned, :] = recv_ref[part, 0:owned, :].astype(F32)
        row = recv_ref[part, owned : owned + 8, :].astype(F32)[0:1, :]
        row = jnp.where(lane < blocks, row, 0.0)
        ids = ids + (pltpu.roll(row, part * blocks, 1) if part else row)
    for b in range(blocks):
        src_ref[b : b + 1, :] = all_ref[pl.ds(pair_ref[0, 1, b], 1), :]
    source = src_ref[...].astype(BF16)
    which = iota((blocks, 128), 0)
    total = jnp.zeros((blocks, 128), F32)
    for b in range(blocks):
        one = dot(source, block_ref[0, b], ((1,), (1,)))
        total = jnp.where(which == b, one, total)
    for part in range(parts):
        out_ref[part] = total.astype(BF16)
    hot = iota(add_ref.shape, 0).astype(F32) == ids
    add_ref[...] = jnp.where(hot, 1.0, 0.0).astype(BF16)


def cubics(g1, g2, g3, g4):
    first = (g4, -(2.0 * g1 * g3 + g2 * g2), 3.0 * g1 * g1 * g2, -(g1 * g1) * (g1 * g1))
    second = (g3, -2.0 * g1 * g2, g1 * g1 * g1)
    third = (g2, -(g1 * g1))
    return first, second, third, (g1,)


def weighted(curves, rows):
    totals = []
    for power in range(4):
        terms = [curve[power] if row is None else curve[power] * row
                 for curve, row in zip(curves, rows) if power < len(curve)]
        totals.append(functools.reduce(lambda x, y: x + y, terms))
    return totals


def wall_body(
    class_ref, inverse_ref, wall_ref, take_ref,
    free_ref, rows_ref, gain_ref, resp_ref, lam_ref, mix_ref, table_ref, take_out, back_out, kind_ref, lhs_ref,
):
    nodes = inverse_ref.shape[1]
    full = functools.partial(
        lax.dot_general,
        dimension_numbers=(((1,), (0,)), ((), ())),
        precision=lax.Precision.HIGHEST,
        preferred_element_type=F32,
    )
    for c in range(inverse_ref.shape[0]):
        one = inverse_ref[c]
        two = full(one, one)
        three = full(two, one)
        four = full(two, two)
        stack = jnp.concatenate(
            [four, one[0:1], two[0:1], three[0:1], jnp.zeros((13, nodes), F32)], axis=0
        )
        high, low = split(stack)
        lhs_ref[c] = jnp.concatenate([high, high, low], axis=1)
        for k, power in enumerate((one, two, three, four)):
            resp_ref[c, k] = jnp.broadcast_to(power[:, 0:1], (nodes, 128))
        curves = cubics(*[resp_ref[c, k, 0:1, :] for k in range(4)])
        for power, value in enumerate(weighted(curves, [None] * 4)):
            table_ref[4 * c + power : 4 * c + power + 1, :] = value

    owned = wall_ref.shape[1]

    def tiles(g, carry):
        base = pl.multiple_of(g * 8, 8)
        firsts = [[], [], [], [], []]
        gains = [[], [], [], []]
        kinds = []
        for q in range(8):
            t = base + q
            kind = class_ref[0, t]
            kinds.append(jnp.full((1, 128), kind, jnp.int32))
            state = wall_ref[0, t]
            high, low = split(state)
            result = dot(lhs_ref[kind], jnp.concatenate([high, low, high], axis=0))
            free_ref[t] = result[0:nodes]
            for k in range(3):
                firsts[k].append(result[nodes + k : nodes + k + 1])
            firsts[3].append(state[0:1])
            firsts[4].append(result[0:1])
            for k in range(4):
                gains[k].append(resp_ref[kind, k, 0:1, :])
        for k in range(5):
            rows_ref[k, pl.ds(base, 8), :] = jnp.concatenate(firsts[k], axis=0)
        for k in range(4):
            gain_ref[k, pl.ds(base, 8), :] = jnp.concatenate(gains[k], axis=0)
        kind_ref[pl.ds(base, 8), :] = jnp.concatenate(kinds, axis=0).astype(F32)
        return carry

    lax.fori_loop(0, owned // 8, tiles, 0, unroll=2)
    curves = cubics(gain_ref[0], gain_ref[1], gain_ref[2], gain_ref[3])
    for power, value in enumerate(weighted(curves, [None] * 4)):
        lam_ref[power] = value
    before = [rows_ref[3], rows_ref[0], rows_ref[1], rows_ref[2]]
    for power, value in enumerate(weighted(curves, before)):
        mix_ref[power] = value
    take = take_ref[...]
    col = column(take.astype(F32), owned).astype(jnp.int32)
    lanes = iota((owned, 2 * owned), 1)
    place = (col & 1) * owned + (col >> 1)
    take_out[...] = jnp.where(lanes == place, 1.0, 0.0).astype(BF16)
    wanted = iota((2 * owned, owned), 0)
    wanted = jnp.where(wanted < owned, 2 * wanted, 2 * (wanted - owned) + 1)
    back_out[...] = jnp.where(take == wanted, 1.0, 0.0).astype(BF16)


def blend_body(refl_ref, add_ref, rows_ref, lam_ref, mix_ref, kind_ref, back_ref, fwd_ref, out_ref, rad_ref, list_ref):
    parts, blocks = refl_ref.shape[0], refl_ref.shape[1]
    owned = add_ref.shape[0]
    rad = dot(add_ref[...], refl_ref[...].reshape(parts * blocks, 128))
    rad_ref[...] = rad
    quarter = wall_gain * rad
    poly = [rows_ref[4] + quarter * lam_ref[0]]
    for power in range(1, 4):
        poly.append(quarter * lam_ref[power] - mix_ref[power - 1])
    poly += [-mix_ref[3], kind_ref[...]]
    placed = dot(back_ref[...], jnp.concatenate([p.astype(BF16) for p in poly], axis=1))
    for t in range(4):
        list_ref[pl.ds(t, owned, stride=16), :] = fwd_ref[t]
    for place in range(2):
        for m in range(6):
            value = placed[place * owned : (place + 1) * owned, 128 * m : 128 * m + 128]
            list_ref[pl.ds(4 + 6 * place + m, owned, stride=16), :] = value
    out_ref[...] = list_ref[...].astype(BF16)


def upwind(speed, centre, lower, upper):
    return jnp.maximum(speed, 0.0) * (centre - lower) + jnp.minimum(speed, 0.0) * (upper - centre)


def air_body(
    theta_ref, wind_ref, eddy_ref, zhalo_ref, near_ref, far_ref, send_ref, speed_ref, base_ref, pick_ref, coef_ref
):
    slots = send_ref.shape[1]
    col = column(send_ref[...].astype(F32), slots)
    live = col >= 0.0
    whole = col.astype(jnp.int32)
    place = jnp.where(live, (whole & 1) * (slots // 2) + (whole >> 1), -1)
    pick_ref[...] = jnp.where(iota((slots, slots), 1) == place, 1.0, 0.0).astype(BF16)
    coef_ref[...] = jnp.where(live, 0.5 + speed_ref[...], 0.0)
    level = lax.axis_index("gz")
    parts = zhalo_ref.shape[0]

    def plane(from_part, valid):
        value = zhalo_ref[jnp.clip(from_part, 0, parts - 1)].astype(F32)
        value = jnp.concatenate([value[4 * q : 4 * q + 4] for q in range(4)], axis=1)
        return jnp.where(valid, value, 0.0)

    below = plane(level - 1, level > 0)
    above = plane(level + 1, level < parts - 1)
    even = lax.axis_index("xy") % 2 == 0
    for k in range(2):
        before = jnp.where(even, far_ref[k], near_ref[k])
        after = jnp.where(even, near_ref[k], far_ref[k])
        c = theta_ref[k]
        lower_z = theta_ref[0] if k else below
        upper_z = above if k else theta_ref[1]
        lower_x = jnp.concatenate([before, c[0:3]], axis=0)
        upper_x = jnp.concatenate([c[1:4], after], axis=0)
        lower_y = jnp.concatenate([c[:, -1:], c[:, :-1]], axis=1)
        upper_y = jnp.concatenate([c[:, 1:], c[:, :1]], axis=1)
        advect = (
            upwind(wind_ref[0, k], c, lower_z, upper_z)
            + upwind(wind_ref[1, k], c, lower_x, upper_x)
            + upwind(wind_ref[2, k], c, lower_y, upper_y)
        )
        laplace = lower_z + upper_z + lower_x + upper_x + lower_y + upper_y - 6.0 * c
        base_ref[k] = c - advect + eddy_ref[k] * laplace


def close_body(
    class_ref, recv_ref, take_ref, rows_ref, gain_ref, rad_ref, free_ref, resp_ref,
    pick_ref, air_ref, coef_ref, table_ref, cell_ref, base_ref,
    wall_hbm, out_ref, list_ref, force_ref, wall_ref, flux_ref, acc_ref, sem,
):
    list_ref[...] = recv_ref[...].astype(F32)
    owned = rad_ref.shape[0]

    def part(t):
        return list_ref[pl.ds(t, owned, stride=16), :].astype(BF16)

    taken = jnp.concatenate(
        [jnp.concatenate([part(0), part(1)], axis=0), jnp.concatenate([part(2), part(3)], axis=0)], axis=1
    )
    taken = dot(take_ref[...], taken)
    air = taken[:, :128]
    quarter = wall_gain * (0.5 + taken[:, 128:])
    rad = wall_gain * rad_ref[...]
    g1, g2, g3 = gain_ref[0], gain_ref[1], gain_ref[2]
    f0 = quarter * (air - rows_ref[3]) + rad
    f1 = quarter * (air - (rows_ref[0] + g1 * f0)) + rad
    f2 = quarter * (air - (rows_ref[1] + (g2 * f0 + g1 * f1))) + rad
    f3 = quarter * (air - (rows_ref[2] + (g3 * f0 + g2 * f1 + g1 * f2))) + rad
    force_ref[0] = f0
    force_ref[1] = f1
    force_ref[2] = f2
    force_ref[3] = f3

    def tile(t, carry):
        kind = class_ref[0, t]
        value = free_ref[t]
        for k in range(4):
            value = value + resp_ref[kind, 3 - k] * force_ref[k, pl.ds(t, 1), :]
        wall_ref[0, t] = value
        return carry

    lax.fori_loop(0, owned, tile, 0, unroll=4)
    copy = pltpu.make_async_copy(wall_ref, wall_hbm, sem)
    copy.start()

    slots = cell_ref.shape[0]
    back = [jnp.concatenate([part(4 + m), part(10 + m)], axis=0) for m in range(6)]
    back = dot(pick_ref[...], jnp.concatenate(back, axis=1))
    poly = [back[:, 128 * m : 128 * m + 128] for m in range(6)]
    own_air, own_coef = air_ref[...], coef_ref[...]
    h = wall_gain * own_coef
    lam = jnp.zeros((slots, 128), F32)
    for c in range(table_ref.shape[0] // 4):
        one = [table_ref[4 * c + power : 4 * c + power + 1, :] for power in range(4)]
        lam = jnp.where(poly[5] == float(c), one[0] + h * (one[1] + h * (one[2] + h * one[3])), lam)
    surface = poly[0] + h * (poly[1] + h * (poly[2] + h * (poly[3] + h * poly[4]))) + h * own_air * lam
    flux_ref[...] = own_coef * (surface - own_air)
    count = 8
    lanes = iota((128, count * 128), 0).astype(BF16)
    lines = iota((32, count * 128), 0).astype(BF16)
    acc_ref[...] = jnp.zeros_like(acc_ref)

    def flat(rows):
        return jnp.concatenate([rows[i : i + 1] for i in range(count)], axis=1)

    def group(p, carry):
        base = pl.multiple_of(p * count, count)
        cells = cell_ref[pl.ds(base, count), :]
        lane = flat((cells & 127).astype(F32)).astype(BF16)
        line = flat((((cells >> 7) & 3) * 8 + (cells >> 9)).astype(F32)).astype(BF16)
        high, low = split(flat(flux_ref[pl.ds(base, count), :]))
        hot = jnp.where(lanes == lane, BF16(1), BF16(0))
        here = lines == line
        placed = jnp.concatenate([jnp.where(here, high, BF16(0)), jnp.where(here, low, BF16(0))], axis=0)
        acc_ref[...] += dot(hot, placed, ((1,), (1,)))
        return carry

    lax.fori_loop(0, slots // count, group, 0, unroll=8)
    heat = acc_ref[...].T
    heat = heat[0:32] + heat[32:64]
    heat = jnp.concatenate([heat[8 * q : 8 * q + 8] for q in range(4)], axis=1)
    for k in range(2):
        out_ref[k] = base_ref[k] + flux_gain * heat[4 * k : 4 * k + 4]
    copy.wait()


def on_device(
    potential_temp,
    wind_field,
    eddy_diff,
    facade_cell,
    tile_send,
    tile_take,
    wall_temp,
    wall_class,
    wall_inverse,
    refl_block,
    refl_pair,
):
    slots = facade_cell.shape[1]
    owned = tile_take.shape[1]
    nodes = wall_temp.shape[2]
    classes = wall_inverse.shape[0]
    blocks = refl_block.shape[1]
    parts = lax.axis_size("gz")
    xy_count = lax.axis_size("xy")
    cells = facade_cell.reshape(slots, 128)
    dma = pltpu.SemaphoreType.DMA

    (payload,) = call(
        pack_body,
        [HBM] * 3,
        [sds((parts, owned + 24, 128), BF16)],
        (wall_temp, refl_pair, potential_temp),
        [
            pltpu.VMEM((owned, 128), F32),
            pltpu.VMEM(refl_pair.shape, jnp.int32),
            pltpu.VMEM(potential_temp.shape, F32),
            pltpu.VMEM((8, 128), F32),
            pltpu.VMEM((2, 16, 128), F32),
            dma((3,)),
        ],
        limit=FULL,
    )
    district = lax.all_to_all(payload, "gz", split_axis=0, concat_axis=0, tiled=True)

    air, speed, forward, pair = call(
        lookup_body,
        [VMEM] * 5,
        [
            sds((slots, 128), F32),
            sds((slots, 128), F32),
            sds((4, slots // 2, 128), F32),
            sds(refl_pair.shape, jnp.int32),
        ],
        (potential_temp, wind_field, cells, tile_send, refl_pair),
        [pltpu.VMEM((32, 128), F32), pltpu.VMEM((32, 128), F32)],
        flops=2 * 48 * 256 * slots * 128,
    )
    row4 = sds((4, owned, 128), F32)
    free, rows, gain, resp, lam, mix, table, take_pick, back_pick, kind = call(
        wall_body,
        [SMEM] + [VMEM] * 3,
        [
            sds((owned, nodes, 128), F32),
            sds((5, owned, 128), F32),
            row4,
            sds((classes, 4, nodes, 128), F32),
            row4,
            row4,
            sds((4 * classes, 128), F32),
            sds((owned, 2 * owned), BF16),
            sds((2 * owned, owned), BF16),
            sds((owned, 128), F32),
        ],
        (wall_class, wall_inverse, wall_temp, tile_take),
        [pltpu.VMEM((classes, nodes + 16, 3 * nodes), BF16)],
        flops=2 * 48 * 96 * owned * 128,
    )
    district, forward, mix = lax.optimization_barrier((district, forward, mix))
    contrib, add_matrix = call(
        reflect_body,
        [SMEM, VMEM, VMEM],
        [sds((parts, blocks, 128), BF16), sds((owned, 128), BF16)],
        (pair, district, refl_block),
        [pltpu.VMEM((parts * owned, 128), F32), pltpu.VMEM((blocks, 128), F32)],
    )
    reflected = lax.all_to_all(contrib, "gz", split_axis=0, concat_axis=0, tiled=True)

    even = lax.axis_index("xy") % 2 == 0
    first_row, last_row = potential_temp[:, 0:1, :], potential_temp[:, 3:4, :]
    mates = [(i, i + 1) for i in range(0, xy_count, 2)]
    others = [(i, i + 1) for i in range(1, xy_count - 1, 2)]
    near = lax.ppermute(jnp.where(even, last_row, first_row), "xy", mates + [(j, i) for i, j in mates])
    far = lax.ppermute(jnp.where(even, first_row, last_row), "xy", others + [(j, i) for i, j in others])

    send_list, rad = call(
        blend_body,
        [VMEM] * 8,
        [sds((16 * xy_count, 128), BF16), sds((owned, 128), F32)],
        (reflected, add_matrix, rows, lam, mix, kind, back_pick, forward),
        [pltpu.VMEM((16 * xy_count, 128), F32)],
    )
    received = lax.all_to_all(send_list, "xy", split_axis=0, concat_axis=0, tiled=True)
    base, pick, coef = call(
        air_body,
        [VMEM] * 8,
        [sds(potential_temp.shape, F32), sds((slots, slots), BF16), sds((slots, 128), F32)],
        (
            potential_temp, wind_field, eddy_diff, district[:, owned + 8 : owned + 24, :], near, far,
            tile_send, speed,
        ),
    )
    wall_next, temp_next = call(
        close_body,
        [SMEM] + [VMEM] * 13,
        [sds((1, owned, nodes, 128), F32), sds(potential_temp.shape, F32)],
        (
            wall_class, received, take_pick, rows, gain, rad, free, resp,
            pick, air, coef, table, cells, base,
        ),
        [
            pltpu.VMEM((16 * xy_count, 128), F32),
            pltpu.VMEM((4, owned, 128), F32),
            pltpu.VMEM((1, owned, nodes, 128), F32),
            pltpu.VMEM((slots, 128), F32),
            pltpu.VMEM((128, 64), F32),
            dma,
        ],
        flops=2 * 64 * 128 * slots * 128,
        out_specs=(pl.BlockSpec(memory_space=pl.ANY), VMEM),
    )
    return temp_next, wall_next


def solution(mesh):
    in_specs = (
        P("gz", "xy", None),
        P(None, "gz", "xy", None),
        P("gz", "xy", None),
        P("gz", "xy", None),
        P("gz", "xy"),
        P("gz", "xy"),
        P("gz", "xy", None, None),
        P("gz", "xy"),
        P(),
        P("xy", "gz", None, None),
        P("xy", None, "gz"),
    )
    out_specs = (P("gz", "xy", None), P("gz", "xy", None, None))
    return jax.shard_map(on_device, mesh=mesh, in_specs=in_specs, out_specs=out_specs, check_vma=False)
```
